128 devices in a mesh: depth: 8 (over x, core), width: 16 (over y, z).
Axes of the slice: x: 4, y: 4, z: 4, core: 2. Of those that a mesh axis runs over, the one named last changes fastest.
Arguments:
- thermal_field: float32 [128, 256, 2048], P('depth', None, 'width'), may hold values from 1 to 3
- particulate_fraction: bfloat16 [128, 256, 2048], P('depth', None, 'width'), may hold values from 0 to 1
- sootiness_extinction: float32 [8], replicated, may hold values from 0.02 to 0.3
- vapour_extinction_rate: float32 [8], replicated, may hold values from 0.02 to 0.2
- planck_over_wavelength: float32 [8], replicated, may hold values from 2 to 8
- layer_sightline_position: int32 [8], replicated, may hold values from 0 to 7, each once
- picture_adjoint_seed: float32 [8, 256, 2048], P(None, ('depth', 'width')), may hold values from -6 to 6
Outputs:
- radiance: float32 [8, 256, 2048], P(None, ('depth', 'width'))
- temperature_gradient: float32 [128, 256, 2048], P('depth', None, 'width')
The draws below stay inside these ranges and needn't reach their ends.
Inputs may be any that keep to these rules, and one draw needn't show every extreme that they name: `layer_sightline_position`: each slab position occurs exactly once.
All inputs are finite; a program needn't handle non-finite values.
Results may differ from the reference program's by a relative error of at most 0.0003.
Values sent between devices are 32-bit elements; how exact they have to be, the bound alone decides.
A program may use at most 192 MiB of HBM per device.

```python
import math
import jax
import jax.numpy as jnp
from jax import lax

NB = 8
CD = 16
PICTURE_HEIGHT = 256
SLABS = 8
SIGHTLINE_STEPS = 128
PICTURE_SPAN = 2048


def block_levels(own_key, extent, pieces, low, largest):
    loudness = 1.0
    for dim, blocks in pieces:
        steps = jax.random.uniform(jax.random.fold_in(jax.random.fold_in(own_key, 6), dim), (blocks,), jnp.float32, low / len(pieces), largest / len(pieces))
        loudness = loudness * jnp.repeat(jnp.exp(steps), extent[dim] // blocks).reshape((-1,) + (1,) * (len(extent) - 1 - dim))
    return loudness


def gaussian(own_key, dims, deviation, limit, shards=(), kind=jnp.bfloat16):
    entries = deviation * jax.random.normal(own_key, dims, jnp.float32)
    if shards:
        entries = entries * block_levels(own_key, dims, shards, -0.22, 0.18)
    return jnp.clip(entries, -limit, limit).astype(kind)


def setup_inputs(seed: int = 0) -> dict:
    arg_keys = jax.random.split(jax.random.key(seed), 8)
    thermal_field = jnp.clip(1.0 + 2.0 * jax.random.uniform(arg_keys[0], (SIGHTLINE_STEPS, PICTURE_HEIGHT, PICTURE_SPAN), jnp.float32) ** block_levels(arg_keys[0], (SIGHTLINE_STEPS, PICTURE_HEIGHT, PICTURE_SPAN), ((0, 8), (2, 16)), -0.2, 0.2), 1.0, 3.0)
    particulate_fraction = jnp.clip(1.0 * jax.random.uniform(arg_keys[1], (SIGHTLINE_STEPS, PICTURE_HEIGHT, PICTURE_SPAN), jnp.float32) ** block_levels(arg_keys[1], (SIGHTLINE_STEPS, PICTURE_HEIGHT, PICTURE_SPAN), ((0, 8), (2, 16)), -0.2, 0.2), 0.0, 1.0).astype(jnp.bfloat16)
    sootiness_extinction = jnp.clip(jnp.exp(jax.random.uniform(arg_keys[2], (NB,), jnp.float32, math.log(0.02), math.log(0.3))), 0.02, 0.3)
    vapour_extinction_rate = jnp.clip(jnp.exp(jax.random.uniform(arg_keys[3], (NB,), jnp.float32, math.log(0.02), math.log(0.2))), 0.02, 0.2)
    planck_over_wavelength = jnp.clip(jnp.exp(jax.random.uniform(arg_keys[4], (NB,), jnp.float32, math.log(2.0), math.log(8.0))), 2.0, 8.0)
    layer_sightline_position = jax.random.permutation(arg_keys[5], SLABS).astype(jnp.int32)
    picture_adjoint_seed = gaussian(arg_keys[6], (NB, PICTURE_HEIGHT, PICTURE_SPAN), 1.0, 6.0, ((1, 128),), jnp.float32)
    return dict(thermal_field=thermal_field, particulate_fraction=particulate_fraction, sootiness_extinction=sootiness_extinction, vapour_extinction_rate=vapour_extinction_rate, planck_over_wavelength=planck_over_wavelength, layer_sightline_position=layer_sightline_position, picture_adjoint_seed=picture_adjoint_seed)


precise = lax.Precision.HIGHEST


def spectral_fields(absolute_heat_level, particulate_field, particulate_multiplier, vapour_multiplier, spectral_multiplier, below_diagonal_matrix):
    sightline_length = absolute_heat_level.shape[1]
    extinction_integral = (particulate_multiplier * particulate_field + vapour_multiplier * absolute_heat_level) / sightline_length
    optical_before = jnp.einsum('kl,slq->skq', below_diagonal_matrix, extinction_integral, precision=precise)
    dimming_factor = jnp.exp(-optical_before)
    blocking_share = 1.0 - jnp.exp(-extinction_integral)
    planck_exponential = jnp.exp(spectral_multiplier / absolute_heat_level)
    emitter_term = (jnp.exp(0.5 * spectral_multiplier) - 1.0) / (planck_exponential - 1.0)
    emitter_derivative = emitter_term * planck_exponential / (planck_exponential - 1.0) * spectral_multiplier / (absolute_heat_level * absolute_heat_level)
    return extinction_integral, dimming_factor, blocking_share, emitter_term, emitter_derivative


def compose(lights, depths, order):
    in_front = (order[:, None] < order[None, :]).astype(jnp.float32)
    lies_behind = order[:, None] > order[None, :]
    optical_before = jnp.einsum('jq,js->sq', depths, in_front, precision=precise)
    dimming_factor = jnp.exp(-optical_before)
    radiance = jnp.sum(dimming_factor * lights, axis=0)
    spacing = optical_before[:, None, :] - optical_before[None, :, :] - depths[None, :, :]
    behind_mask = lies_behind[:, :, None]
    weight = jnp.where(behind_mask, jnp.exp(-jnp.where(behind_mask, spacing, 0.0)), 0.0)
    behind_light = jnp.sum(weight * lights[:, None, :], axis=0)
    return radiance, dimming_factor, behind_light


def reference(thermal_field, particulate_fraction, sootiness_extinction, vapour_extinction_rate, planck_over_wavelength, layer_sightline_position, picture_adjoint_seed):
    layer_total = SLABS
    sightline_length = CD
    picture_entries = PICTURE_HEIGHT * PICTURE_SPAN
    absolute_heat_level = thermal_field.reshape(layer_total, sightline_length, picture_entries)
    particulate_field = particulate_fraction.astype(jnp.float32).reshape(layer_total, sightline_length, picture_entries)
    below_diagonal_matrix = jnp.tril(jnp.ones((sightline_length, sightline_length), jnp.float32), -1)
    strict_upper = below_diagonal_matrix.T
    cotangent = picture_adjoint_seed.reshape(NB, picture_entries)

    def march_band(gradient, inputs):
        particulate_multiplier, vapour_multiplier, spectral_multiplier, tangent = inputs
        extinction_integral, dimming_factor, blocking_share, emitter_term, emitter_derivative = spectral_fields(absolute_heat_level, particulate_field, particulate_multiplier, vapour_multiplier, spectral_multiplier, below_diagonal_matrix)
        emitted = dimming_factor * blocking_share * emitter_term
        lights = jnp.sum(emitted, axis=1)
        depths = jnp.sum(extinction_integral, axis=1)
        radiance, front_fade, behind_light = compose(lights, depths, layer_sightline_position)
        seen_weight = tangent[None, :] * front_fade
        far_weight = seen_weight * behind_light
        emitted_after = jnp.einsum('kl,slq->skq', strict_upper, emitted, precision=precise)
        gas_rate = vapour_multiplier / sightline_length
        addend = seen_weight[:, None, :] * (dimming_factor * blocking_share * emitter_derivative + (dimming_factor * jnp.exp(-extinction_integral) * emitter_term - emitted_after) * gas_rate) - (far_weight * jnp.exp(-depths))[:, None, :] * gas_rate
        return gradient + addend, radiance

    gradient, radiance = lax.scan(march_band, jnp.zeros((layer_total, sightline_length, picture_entries), jnp.float32), (sootiness_extinction, vapour_extinction_rate, planck_over_wavelength, cotangent))
    return radiance.reshape(NB, PICTURE_HEIGHT, PICTURE_SPAN), gradient.reshape(SIGHTLINE_STEPS, PICTURE_HEIGHT, PICTURE_SPAN)
```

```python
import math

import jax
import jax.numpy as jnp
from jax import lax
from jax.experimental import pallas as pl
from jax.experimental.pallas import tpu as pltpu
from jax.sharding import PartitionSpec as P

NB = 8
CD = 16
SLABS = 8
ROWS = 32
LANES = 128
LOG2E = math.log2(math.e)
VMEM = pltpu.CompilerParams(vmem_limit_bytes=48 << 20)


def light_kernel(co, t_ref, p_ref, out_ref, pf):
    for k in range(CD):
        pf[k] = p_ref[k].astype(jnp.float32)

    @pl.loop(0, ROWS // 8)
    def _(i):
        rows = pl.ds(pl.multiple_of(i * 8, 8), 8)
        pp = jnp.zeros((8, LANES), jnp.float32)
        tt = jnp.zeros((8, LANES), jnp.float32)
        before = [jnp.ones((8, LANES), jnp.float32)] * NB
        light = [jnp.zeros((8, LANES), jnp.float32)] * NB
        for k in range(CD):
            t = t_ref[k, rows, :]
            pp = pp + pf[k, rows, :]
            tt = tt + t
            inv = 1.0 / t
            for b in range(NB):
                r = 1.0 / (jnp.exp2(co[2, b] * inv) - 1.0)
                behind = jnp.exp2(co[0, b] * pp + co[1, b] * tt)
                light[b] = light[b] + (before[b] - behind) * r
                before[b] = behind
        for b in range(NB):
            out_ref[b, rows, :] = light[b] * co[5, b]
        out_ref[NB, rows, :] = pp
        out_ref[NB + 1, rows, :] = tt


def grad_kernel(co, t_ref, p_ref, w_ref, g_ref, pf):
    for k in range(CD):
        pf[k] = p_ref[k].astype(jnp.float32)

    @pl.loop(0, ROWS // 8)
    def _(i):
        rows = pl.ds(pl.multiple_of(i * 8, 8), 8)
        pp = jnp.zeros((8, LANES), jnp.float32)
        tt = jnp.zeros((8, LANES), jnp.float32)
        before = [jnp.ones((8, LANES), jnp.float32)] * NB
        y = [jnp.zeros((8, LANES), jnp.float32)] * NB
        last = [jnp.zeros((8, LANES), jnp.float32)] * NB
        seen = [w_ref[b, rows, :] for b in range(NB)]
        w1 = [seen[b] * co[3, b] for b in range(NB)]
        w2 = [seen[b] * co[4, b] for b in range(NB)]
        q = w_ref[NB, rows, :]
        for k in range(CD):
            t = t_ref[k, rows, :]
            pp = pp + pf[k, rows, :]
            tt = tt + t
            inv = 1.0 / t
            s = -q
            v = jnp.zeros((8, LANES), jnp.float32)
            for b in range(NB):
                r = 1.0 / (jnp.exp2(co[2, b] * inv) - 1.0)
                behind = jnp.exp2(co[0, b] * pp + co[1, b] * tt)
                y[b] = y[b] + before[b] * (r - last[b])
                x = (before[b] - behind) * (r * (r + 1.0))
                s = s + w1[b] * y[b]
                v = v + w2[b] * x
                before[b] = behind
                last[b] = r
            g_ref[k, rows, :] = s + v * (inv * inv)


def compose_kernel(pos, co, got_ref, seed_ref, rad_ref, back_ref):
    front = [
        [jnp.where(pos[i] < pos[j], 1.0, 0.0) for j in range(SLABS)] for i in range(SLABS)
    ]

    @pl.loop(0, ROWS // 8)
    def _(i):
        rows = pl.ds(pl.multiple_of(i * 8, 8), 8)
        ps = [got_ref[NB, s, rows, :] for s in range(SLABS)]
        ts = [got_ref[NB + 1, s, rows, :] for s in range(SLABS)]
        pp = [sum(front[a][s] * ps[a] for a in range(SLABS) if a != s) for s in range(SLABS)]
        tt = [sum(front[a][s] * ts[a] for a in range(SLABS) if a != s) for s in range(SLABS)]
        q = [jnp.zeros((8, LANES), jnp.float32)] * SLABS
        for b in range(NB):
            seed = seed_ref[b, rows, :]
            weight = seed * co[6, b]
            faded = []
            for s in range(SLABS):
                dim = jnp.exp2(co[0, b] * pp[s] + co[1, b] * tt[s])
                back_ref[b, s, rows, :] = seed * dim
                faded.append(dim * got_ref[b, s, rows, :])
            rad_ref[b, rows, :] = sum(faded)
            for s in range(SLABS):
                rest = faded[s]
                for a in range(SLABS):
                    if a != s:
                        rest = rest + front[s][a] * faded[a]
                q[s] = q[s] + weight * rest
        for s in range(SLABS):
            back_ref[NB, s, rows, :] = q[s]


def on_device(
    thermal_field,
    particulate_fraction,
    sootiness_extinction,
    vapour_extinction_rate,
    planck_over_wavelength,
    layer_sightline_position,
    picture_adjoint_seed,
):
    gas = vapour_extinction_rate / CD
    scale = jnp.exp(0.5 * planck_over_wavelength) - 1.0
    co = jnp.stack(
        [
            sootiness_extinction * (-LOG2E / CD),
            vapour_extinction_rate * (-LOG2E / CD),
            planck_over_wavelength * LOG2E,
            scale * gas,
            scale * planck_over_wavelength,
            scale,
            gas,
        ]
    )
    f32 = jnp.float32
    lines = thermal_field.shape[1]
    smem = pl.BlockSpec(memory_space=pltpu.SMEM)
    cells = pl.BlockSpec((CD, ROWS, LANES), lambda i: (0, i, 0))
    sent = pl.pallas_call(
        light_kernel,
        grid=(lines // ROWS,),
        out_shape=jax.ShapeDtypeStruct((NB + 2, lines, LANES), f32),
        in_specs=[smem, cells, cells],
        out_specs=pl.BlockSpec((NB + 2, ROWS, LANES), lambda i: (0, i, 0)),
        scratch_shapes=[pltpu.VMEM((CD, ROWS, LANES), f32)],
        compiler_params=VMEM,
    )(co, thermal_field, particulate_fraction)
    seeds = lax.all_to_all(
        picture_adjoint_seed.reshape(NB, 2, 16, LANES), "width", split_axis=2, concat_axis=1, tiled=True
    ).reshape(NB, ROWS, LANES)
    got = lax.all_to_all(
        sent.reshape(NB + 2, SLABS, ROWS, LANES), "depth", split_axis=1, concat_axis=1, tiled=True
    )
    radiance, back = pl.pallas_call(
        compose_kernel,
        out_shape=(
            jax.ShapeDtypeStruct((NB, ROWS, LANES), f32),
            jax.ShapeDtypeStruct((NB + 1, SLABS, ROWS, LANES), f32),
        ),
        in_specs=[smem, smem] + [pl.BlockSpec(memory_space=pltpu.VMEM)] * 2,
        out_specs=(pl.BlockSpec(memory_space=pltpu.VMEM),) * 2,
        compiler_params=VMEM,
    )(layer_sightline_position, co, got, seeds)
    weights = lax.all_to_all(back, "depth", split_axis=1, concat_axis=1, tiled=True).reshape(
        NB + 1, lines, LANES
    )
    radiance = lax.all_to_all(
        radiance.reshape(NB, ROWS, 1, LANES), "width", split_axis=1, concat_axis=2, tiled=True
    ).reshape(NB, 2, 16 * LANES)
    gradient = pl.pallas_call(
        grad_kernel,
        grid=(lines // ROWS,),
        out_shape=jax.ShapeDtypeStruct((CD, lines, LANES), f32),
        in_specs=[smem, cells, cells, pl.BlockSpec((NB + 1, ROWS, LANES), lambda i: (0, i, 0))],
        out_specs=cells,
        scratch_shapes=[pltpu.VMEM((CD, ROWS, LANES), f32)],
        compiler_params=VMEM,
    )(co, thermal_field, particulate_fraction, weights)
    return radiance, gradient


def solution(mesh):
    placed = (
        P("depth", None, "width"),
        P("depth", None, "width"),
        P(),
        P(),
        P(),
        P(),
        P(None, ("depth", "width"), None),
    )
    return jax.shard_map(
        on_device,
        mesh=mesh,
        in_specs=placed,
        out_specs=(P(None, ("depth", "width"), None), P("depth", None, "width")),
        check_vma=False,
    )
```

```python
import math

import jax
import jax.numpy as jnp
from jax import lax
from jax.experimental import pallas as pl
from jax.experimental.pallas import tpu as pltpu
from jax.sharding import PartitionSpec as P

MESH = pl.DeviceIdType.MESH
NB = 8
CD = 16
SLABS = 8
COLS = 16
CHIPS = 4
LINES = 256
ROWS = 32
LANES = 128
TILE = (8, LANES)
LOG2E = math.log2(math.e)
F32 = jnp.float32


def kernel(
    soot,
    vapour,
    planck,
    pos,
    t_hbm,
    p_hbm,
    seed_hbm,
    rad_out,
    grad_hbm,
    q_out,
    t_v,
    p_v,
    pf,
    big,
    table,
    sum_s,
    sum_r,
    fro_s,
    fro_r,
    seed_l,
    seed_a,
    lit,
    pair_r,
    chip_s,
    chip_r,
    gs_s,
    gs_r,
    q_s,
    q_r,
    rad_v,
    rad_s,
    rad_r,
    grad_v,
    in_sem,
    out_sem,
    sum_ss,
    sum_rs,
    fro_ss,
    fro_rs,
    seed_ss,
    seed_rs,
    sax_ss,
    sax_rs,
    sap_ss,
    sap_rs,
    pair_ss,
    pair_rs,
    chip_ss,
    chip_rs,
    gs_ss,
    gs_rs,
    q_ss,
    q_rs,
    rad_ss,
    rad_rs,
):
    d = lax.axis_index("depth")
    w = lax.axis_index("width")
    c = lax.rem(d, 2)
    x = d // 2
    pair = d + 1 - 2 * c

    def chip(i):
        return lax.rem(x + 1 + i, CHIPS)

    def tile_of(n):
        g = n // 4
        e = 2 * chip(g // 2) + lax.rem(g + 1 + c, 2)
        return e, pl.multiple_of(8 * lax.rem(n, 4), 8)

    def rdma(src, dst, ss, rs, dev):
        return pltpu.make_async_remote_copy(
            src_ref=src, dst_ref=dst, send_sem=ss, recv_sem=rs, device_id=dev, device_id_type=MESH
        )

    def loads(i):
        rows = pl.ds(pl.multiple_of(64 * chip(i), 64), 64)
        return (
            pltpu.make_async_copy(t_hbm.at[:, rows, :], t_v.at[:, rows, :], in_sem.at[0, i]),
            pltpu.make_async_copy(p_hbm.at[:, rows, :], p_v.at[:, rows, :], in_sem.at[1, i]),
        )

    for i in range(CHIPS):
        for cp in loads(i):
            cp.start()

    barrier = pltpu.get_barrier_semaphore()
    for o in range(1, SLABS):
        pl.semaphore_signal(
            barrier, inc=1, device_id={"depth": lax.rem(d + o, SLABS)}, device_id_type=MESH
        )
    for o in range(1, COLS):
        pl.semaphore_signal(
            barrier, inc=1, device_id={"width": lax.rem(w + o, COLS)}, device_id_type=MESH
        )

    ks = [soot[b] * (-LOG2E / CD) for b in range(NB)]
    kv = [vapour[b] * (-LOG2E / CD) for b in range(NB)]
    kp = [planck[b] * LOG2E for b in range(NB)]
    gas = [vapour[b] * (1.0 / CD) for b in range(NB)]
    front = [
        [jnp.where(pos[i] < pos[j], 1.0, 0.0) for j in range(SLABS)] for i in range(SLABS)
    ]
    for b in range(NB):
        scale = jnp.exp(jnp.full(TILE, 0.5 * planck[b], F32)) - 1.0
        table[0, b] = scale
        table[1, b] = scale * gas[b]
        table[2, b] = jnp.full(TILE, planck[b], F32) / gas[b]

    pl.semaphore_wait(barrier, SLABS + COLS - 2)

    def cols(i):
        return pl.ds(pl.multiple_of(i * LANES, LANES), LANES)

    def seed_copy(to, slot):
        return rdma(
            seed_hbm.at[:, cols(to)], seed_l.at[slot], seed_ss.at[to], seed_rs.at[slot], {"width": to}
        )

    @pl.loop(1, COLS)
    def _(o):
        seed_copy(lax.rem(w + o, COLS), w).start()

    seed_own = pltpu.make_async_copy(seed_hbm.at[:, cols(w)], seed_l.at[w], out_sem.at[SLABS])
    seed_own.start()

    def exchange(send, recv, ss, rs):
        def make(to, slot):
            return rdma(send.at[to], recv.at[slot], ss.at[to], rs.at[slot], {"depth": to})

        return make

    sums = exchange(sum_s, sum_r, sum_ss, sum_rs)
    fronts = exchange(fro_s, fro_r, fro_ss, fro_rs)
    grads = exchange(gs_s, gs_r, gs_ss, gs_rs)
    quots = exchange(q_s, q_r, q_ss, q_rs)

    def others():
        return [lax.rem(d + o, SLABS) for o in (2, 3, 4, 5, 6, 7, 1)]

    for i in range(CHIPS):
        for cp in loads(i):
            cp.wait()
        for half in range(2):
            e = 2 * chip(i) + lax.rem(half + 1 + c, 2)

            @pl.loop(0, 2)
            def _(j):
                r16 = pl.multiple_of(16 * j, 16)
                rows = pl.ds(pl.multiple_of(ROWS * e + r16, 16), 16)
                pp = jnp.zeros((16, LANES), F32)
                tt = jnp.zeros((16, LANES), F32)
                for k in range(CD):
                    p = p_v[k, rows, :].astype(F32)
                    pf[k, rows, :] = p
                    pp = pp + p
                    tt = tt + t_v[k, rows, :]
                if i == CHIPS - 1 and half == 1:
                    sum_r[d, 0, pl.ds(r16, 16), :] = pp
                    sum_r[d, 1, pl.ds(r16, 16), :] = tt
                else:
                    sum_s[e, 0, pl.ds(r16, 16), :] = pp
                    sum_s[e, 1, pl.ds(r16, 16), :] = tt

            if not (i == CHIPS - 1 and half == 1):
                sums(e, d).start()

    def heavy(n0, n1):
        @pl.loop(n0, n1)
        def _(n):
            e, r8 = tile_of(n)
            rows = pl.ds(pl.multiple_of(ROWS * e + r8, 8), 8)
            pp = jnp.zeros(TILE, F32)
            tt = jnp.zeros(TILE, F32)
            before = [None] * NB
            y = [None] * NB
            last = [None] * NB
            for k in range(CD):
                t = t_v[k, rows, :]
                pp = pp + pf[k, rows, :]
                tt = tt + t
                inv = 1.0 / t
                inv2 = inv * inv
                for b in range(NB):
                    r = 1.0 / (jnp.exp2(kp[b] * inv) - 1.0)
                    behind = jnp.exp2(ks[b] * pp + kv[b] * tt)
                    if k == 0:
                        y[b] = r
                        lost = 1.0 - behind
                    else:
                        y[b] = y[b] + before[b] * (r - last[b])
                        lost = before[b] - behind
                    big[b, k, rows, :] = y[b] + (lost * (r * (r + 1.0))) * (table[2, b] * inv2)
                    before[b] = behind
                    last[b] = r
            for b in range(NB):
                lit[e, pl.ds(ROWS * b + r8, 8), :] = (y[b] - before[b] * last[b]) * table[0, b]

    def make_fronts():
        for p in others():
            sums(p, p).wait_recv()

        @pl.loop(0, ROWS // 8)
        def _(j):
            rows = pl.ds(pl.multiple_of(8 * j, 8), 8)
            for h in range(2):
                part = [sum_r[s, h, rows, :] for s in range(SLABS)]
                for s in range(SLABS):
                    fro_s[s, h, rows, :] = sum(
                        front[a][s] * part[a] for a in range(SLABS) if a != s
                    )

        fro_r[d] = fro_s[d]
        for p in others():
            fronts(p, d).start()

    def same(i):
        return lax.rem(d + 2 * i, SLABS)

    def sax(to, slot):
        return rdma(
            seed_a.at[slot], seed_a.at[slot], sax_ss.at[to // 2], sax_rs.at[slot // 2], {"depth": to}
        )

    def sap(slot):
        return rdma(
            seed_a.at[slot], seed_a.at[slot], sap_ss.at[slot // 2], sap_rs.at[slot // 2], {"depth": pair}
        )

    def spread_seeds():
        @pl.loop(1, COLS)
        def _(o):
            p = lax.rem(w + o, COLS)
            seed_copy(p, p).wait_recv()

        seed_own.wait()
        for b in range(NB):
            for r in range(2):
                for h in range(2):
                    seed_a[d, pl.ds(ROWS * b + r + 16 * h, 8, stride=2), :] = seed_l[
                        pl.ds(8 * h, 8), 2 * b + r, :
                    ]
        for i in (2, 1, 3):
            sax(same(i), d).start()
        sap(d).start()

    def forward_seeds():
        for i in (1, 3, 2):
            sax(same(i), same(i)).wait_recv()
            sap(same(i)).start()

    def dims(e, r8):
        pp = fro_r[e, 0, pl.ds(r8, 8), :]
        tt = fro_r[e, 1, pl.ds(r8, 8), :]
        return [jnp.exp2(ks[b] * pp + kv[b] * tt) for b in range(NB)]

    def fade(n0, n1):
        @pl.loop(n0, n1)
        def _(n):
            e, r8 = tile_of(n)
            dim = dims(e, r8)
            for b in range(NB):
                rows = pl.ds(ROWS * b + r8, 8)
                lit[e, rows, :] = lit[e, rows, :] * dim[b]

    def pairs(i, slot):
        return rdma(
            lit.at[2 * chip(i) + 1 - c],
            pair_r.at[slot],
            pair_ss.at[i],
            pair_rs.at[slot],
            {"depth": pair},
        )

    def chips(i, slot):
        return rdma(
            chip_s.at[i], chip_r.at[slot], chip_ss.at[i], chip_rs.at[slot], {"depth": same(i + 1)}
        )

    def join(i):
        pairs(i, chip(i)).wait_recv()
        e = 2 * chip(i) + c

        @pl.loop(0, NB * ROWS // 8)
        def _(j):
            rows = pl.ds(pl.multiple_of(8 * j, 8), 8)
            chip_s[i, rows, :] = lit[e, rows, :] + pair_r[chip(i), rows, :]

    heavy(0, 12)
    make_fronts()
    heavy(12, 16)
    spread_seeds()
    heavy(16, 24)
    forward_seeds()
    for p in others():
        fronts(p, p).wait_recv()
    for i in range(3):
        fade(8 * i, 8 * i + 8)
        pairs(i, chip(i)).start()
    heavy(24, 28)
    for i in range(3):
        join(i)
        chips(i, x).start()
    heavy(28, 32)
    fade(24, 32)
    pairs(3, chip(3)).start()

    for s in range(CHIPS):
        sap(2 * s + 1 - c).wait_recv()

    @pl.loop(0, 32)
    def _(n):
        e, r8 = tile_of(n)
        total = jnp.zeros(TILE, F32)
        for b in range(NB):
            rows = pl.ds(ROWS * b + r8, 8)
            total = total + gas[b] * (seed_a[e, rows, :] * lit[e, rows, :])
        gs_s[e, pl.ds(r8, 8), :] = total

    gs_r[d] = gs_s[d]
    for p in others():
        grads(p, d).start()

    def out_copy(g):
        e, _ = tile_of(4 * g)
        rows = pl.ds(pl.multiple_of(ROWS * e, ROWS), ROWS)
        return pltpu.make_async_copy(
            grad_v.at[:, rows, :], grad_hbm.at[:, rows, :], out_sem.at[g]
        )

    def finish(g0, g1):
        @pl.loop(g0, g1)
        def _(g):
            @pl.loop(0, 4)
            def _(j):
                e, r8 = tile_of(4 * g + j)
                rows = pl.ds(pl.multiple_of(ROWS * e + r8, 8), 8)
                dim = dims(e, r8)
                wt = [
                    table[1, b] * (seed_a[e, pl.ds(ROWS * b + r8, 8), :] * dim[b])
                    for b in range(NB)
                ]
                for k in range(CD):
                    acc = wt[0] * big[0, k, rows, :]
                    for b in range(1, NB):
                        acc = acc + wt[b] * big[b, k, rows, :]
                    grad_v[k, rows, :] = acc

            out_copy(g).start()

    finish(0, 4)

    pairs(3, x).wait_recv()
    for i in range(3):
        chips(i, chip(i)).wait_recv()

    @pl.loop(0, NB * ROWS // 8)
    def _(j):
        rows = pl.ds(pl.multiple_of(8 * j, 8), 8)
        rad_v[rows, :] = (
            (lit[d, rows, :] + pair_r[x, rows, :])
            + (chip_r[chip(0), rows, :] + chip_r[chip(1), rows, :])
            + chip_r[chip(2), rows, :]
        )

    for b in range(NB):
        for r in range(2):
            for h in range(2):
                rad_s[pl.ds(8 * h, 8), 2 * b + r, :] = rad_v[
                    pl.ds(ROWS * b + r + 16 * h, 8, stride=2), :
                ]
    rad_r[:, cols(w)] = rad_s[w]

    def rad_copy(to, slot):
        return rdma(
            rad_s.at[to], rad_r.at[:, cols(slot)], rad_ss.at[to], rad_rs.at[slot], {"width": to}
        )

    @pl.loop(1, COLS)
    def _(o):
        rad_copy(lax.rem(w + o, COLS), w).start()

    for p in others():
        grads(p, p).wait_recv()

    @pl.loop(0, ROWS // 8)
    def _(j):
        rows = pl.ds(pl.multiple_of(8 * j, 8), 8)
        part = [gs_r[s, rows, :] for s in range(SLABS)]
        for s in range(SLABS):
            rest = part[s]
            for a in range(SLABS):
                if a != s:
                    rest = rest + front[s][a] * part[a]
            q_s[s, rows, :] = rest

    q_r[d] = q_s[d]
    for p in others():
        quots(p, d).start()
    finish(4, 8)

    for p in others():
        quots(p, p).wait_recv()
    q_out[...] = q_r[...]

    @pl.loop(1, COLS)
    def _(o):
        p = lax.rem(w + o, COLS)
        rad_copy(p, p).wait_recv()

    rad_out[...] = rad_r[...]
    for g in range(SLABS):
        out_copy(g).wait()
    for p in others():
        sums(p, d).wait_send()
        fronts(p, d).wait_send()
        grads(p, d).wait_send()
        quots(p, d).wait_send()
    for i in (1, 2, 3):
        sax(same(i), d).wait_send()
    for s in range(CHIPS):
        sap(2 * s + c).wait_send()
        pairs(s, chip(s)).wait_send()
    for i in range(3):
        chips(i, x).wait_send()

    @pl.loop(1, COLS)
    def _(o):
        p = lax.rem(w + o, COLS)
        seed_copy(p, w).wait_send()
        rad_copy(p, w).wait_send()


def on_device(
    thermal_field,
    particulate_fraction,
    sootiness_extinction,
    vapour_extinction_rate,
    planck_over_wavelength,
    layer_sightline_position,
    picture_adjoint_seed,
):
    smem = pl.BlockSpec(memory_space=pltpu.SMEM)
    vmem = pl.BlockSpec(memory_space=pltpu.VMEM)
    hbm = pl.BlockSpec(memory_space=pl.ANY)

    def v(*shape):
        return pltpu.VMEM(shape, F32)

    def sems(*shape):
        return pltpu.SemaphoreType.DMA(shape)

    field = (CD, LINES, LANES)
    image = (NB * ROWS, LANES)
    radiance, gradient, quot = pl.pallas_call(
        kernel,
        out_shape=(
            jax.ShapeDtypeStruct((2 * NB, COLS * LANES), F32),
            jax.ShapeDtypeStruct(field, F32),
            jax.ShapeDtypeStruct((SLABS, ROWS, LANES), F32),
        ),
        in_specs=[smem, smem, smem, smem, hbm, hbm, hbm],
        out_specs=(vmem, hbm, vmem),
        scratch_shapes=[
            v(*field),
            pltpu.VMEM(field, jnp.bfloat16),
            v(*field),
            v(NB, *field),
            v(3, NB, *TILE),
            v(SLABS, 2, ROWS, LANES),
            v(SLABS, 2, ROWS, LANES),
            v(SLABS, 2, ROWS, LANES),
            v(SLABS, 2, ROWS, LANES),
            v(COLS, 2 * NB, LANES),
            v(SLABS, *image),
            v(SLABS, *image),
            v(CHIPS, *image),
            v(3, *image),
            v(CHIPS, *image),
            v(SLABS, ROWS, LANES),
            v(SLABS, ROWS, LANES),
            v(SLABS, ROWS, LANES),
            v(SLABS, ROWS, LANES),
            v(*image),
            v(COLS, 2 * NB, LANES),
            v(2 * NB, COLS * LANES),
            v(*field),
            sems(2, CHIPS),
            sems(SLABS + 1),
            sems(SLABS),
            sems(SLABS),
            sems(SLABS),
            sems(SLABS),
            sems(COLS),
            sems(COLS),
            sems(CHIPS),
            sems(CHIPS),
            sems(CHIPS),
            sems(CHIPS),
            sems(CHIPS),
            sems(CHIPS),
            sems(3),
            sems(CHIPS),
            sems(SLABS),
            sems(SLABS),
            sems(SLABS),
            sems(SLABS),
            sems(COLS),
            sems(COLS),
        ],
        compiler_params=pltpu.CompilerParams(
            collective_id=0, has_side_effects=True, vmem_limit_bytes=56 << 20
        ),
    )(
        sootiness_extinction,
        vapour_extinction_rate,
        planck_over_wavelength,
        layer_sightline_position,
        thermal_field,
        particulate_fraction,
        picture_adjoint_seed.reshape(2 * NB, COLS * LANES),
    )
    return (
        radiance.reshape(NB, 2, COLS * LANES),
        gradient - quot.reshape(1, LINES, LANES),
    )


def solution(mesh):
    placed = (
        P("depth", None, "width"),
        P("depth", None, "width"),
        P(),
        P(),
        P(),
        P(),
        P(None, ("depth", "width"), None),
    )
    return jax.shard_map(
        on_device,
        mesh=mesh,
        in_specs=placed,
        out_specs=(P(None, ("depth", "width"), None), P("depth", None, "width")),
        check_vma=False,
    )
```

```python
import math

import jax
import jax.numpy as jnp
from jax import lax
from jax.experimental import pallas as pl
from jax.experimental.pallas import tpu as pltpu
from jax.sharding import PartitionSpec as P

MESH = pl.DeviceIdType.MESH
NB = 8
CD = 16
SLABS = 8
COLS = 16
CHIPS = 4
LINES = 256
ROWS = 32
LANES = 128
TILE = (8, LANES)
LOG2E = math.log2(math.e)
F32 = jnp.float32


def kernel(
    soot,
    vapour,
    planck,
    pos,
    t_hbm,
    p_hbm,
    seed_hbm,
    rad_out,
    grad_hbm,
    q_out,
    t_v,
    p_v,
    pf,
    big,
    table,
    sum_s,
    sum_r,
    fro_s,
    fro_r,
    seed_l,
    seed_a,
    lit,
    pair_r,
    chip_s,
    chip_r,
    gs_s,
    gs_r,
    q_s,
    q_r,
    rad_v,
    rad_s,
    rad_r,
    grad_v,
    in_sem,
    out_sem,
    sum_ss,
    sum_rs,
    fro_ss,
    fro_rs,
    seed_ss,
    seed_rs,
    sax_ss,
    sax_rs,
    sap_ss,
    sap_rs,
    pair_ss,
    pair_rs,
    chip_ss,
    chip_rs,
    gs_ss,
    gs_rs,
    q_ss,
    q_rs,
    rad_ss,
    rad_rs,
):
    d = lax.axis_index("depth")
    w = lax.axis_index("width")
    c = lax.rem(d, 2)
    x = d // 2
    pair = d + 1 - 2 * c

    def chip(i):
        return lax.rem(x + 1 + i, CHIPS)

    def tile_of(n):
        g = n // 4
        e = 2 * chip(g // 2) + lax.rem(g + 1 + c, 2)
        return e, pl.multiple_of(8 * lax.rem(n, 4), 8)

    def rdma(src, dst, ss, rs, dev):
        return pltpu.make_async_remote_copy(
            src_ref=src, dst_ref=dst, send_sem=ss, recv_sem=rs, device_id=dev, device_id_type=MESH
        )

    def loads(i):
        rows = pl.ds(pl.multiple_of(64 * chip(i), 64), 64)
        return (
            pltpu.make_async_copy(t_hbm.at[:, rows, :], t_v.at[:, rows, :], in_sem.at[0, i]),
            pltpu.make_async_copy(p_hbm.at[:, rows, :], p_v.at[:, rows, :], in_sem.at[1, i]),
        )

    for i in range(CHIPS):
        for cp in loads(i):
            cp.start()

    barrier = pltpu.get_barrier_semaphore()
    for o in range(1, SLABS):
        pl.semaphore_signal(
            barrier, inc=1, device_id={"depth": lax.rem(d + o, SLABS)}, device_id_type=MESH
        )
    for o in range(1, COLS):
        pl.semaphore_signal(
            barrier, inc=1, device_id={"width": lax.rem(w + o, COLS)}, device_id_type=MESH
        )

    ks = [soot[b] * (-LOG2E / CD) for b in range(NB)]
    kv = [vapour[b] * (-LOG2E / CD) for b in range(NB)]
    kp = [planck[b] * LOG2E for b in range(NB)]
    gas = [vapour[b] * (1.0 / CD) for b in range(NB)]
    front = [
        [jnp.where(pos[i] < pos[j], 1.0, 0.0) for j in range(SLABS)] for i in range(SLABS)
    ]
    for b in range(NB):
        scale = jnp.exp(jnp.full(TILE, 0.5 * planck[b], F32)) - 1.0
        table[0, b] = scale
        table[1, b] = scale * gas[b]
        table[2, b] = jnp.full(TILE, planck[b], F32) / gas[b]

    def cols(i):
        return pl.ds(pl.multiple_of(i * LANES, LANES), LANES)

    def seed_copy(to, slot):
        return rdma(
            seed_hbm.at[:, :, cols(to)], seed_l.at[slot], seed_ss.at[to], seed_rs.at[slot], {"width": to}
        )

    seed_own = pltpu.make_async_copy(seed_hbm.at[:, :, cols(w)], seed_l.at[w], out_sem.at[SLABS])
    seed_own.start()

    def exchange(send, recv, ss, rs):
        def make(to, slot):
            return rdma(send.at[to], recv.at[slot], ss.at[to], rs.at[slot], {"depth": to})

        return make

    sums = exchange(sum_s, sum_r, sum_ss, sum_rs)
    fronts = exchange(fro_s, fro_r, fro_ss, fro_rs)
    grads = exchange(gs_s, gs_r, gs_ss, gs_rs)
    quots = exchange(q_s, q_r, q_ss, q_rs)

    def others():
        return [lax.rem(d + o, SLABS) for o in (2, 3, 4, 5, 6, 7, 1)]

    for i in range(CHIPS):
        for cp in loads(i):
            cp.wait()
        for half in range(2):
            e = 2 * chip(i) + lax.rem(half + 1 + c, 2)

            @pl.loop(0, 2)
            def _(j):
                r16 = pl.multiple_of(16 * j, 16)
                rows = pl.ds(pl.multiple_of(ROWS * e + r16, 16), 16)
                pp = jnp.zeros((16, LANES), F32)
                tt = jnp.zeros((16, LANES), F32)
                for k in range(CD):
                    p = p_v[k, rows, :].astype(F32)
                    pf[k, rows, :] = p
                    pp = pp + p
                    tt = tt + t_v[k, rows, :]
                if i == CHIPS - 1 and half == 1:
                    sum_r[d, 0, pl.ds(r16, 16), :] = pp
                    sum_r[d, 1, pl.ds(r16, 16), :] = tt
                else:
                    sum_s[e, 0, pl.ds(r16, 16), :] = pp
                    sum_s[e, 1, pl.ds(r16, 16), :] = tt


    def heavy(n0, n1):
        @pl.loop(n0, n1)
        def _(n):
            e, r8 = tile_of(n)
            rows = pl.ds(pl.multiple_of(ROWS * e + r8, 8), 8)
            pp = jnp.zeros(TILE, F32)
            tt = jnp.zeros(TILE, F32)
            before = [None] * NB
            y = [None] * NB
            last = [None] * NB
            for k in range(CD):
                t = t_v[k, rows, :]
                pp = pp + pf[k, rows, :]
                tt = tt + t
                inv = 1.0 / t
                inv2 = inv * inv
                for b in range(NB):
                    r = 1.0 / (jnp.exp2(kp[b] * inv) - 1.0)
                    behind = jnp.exp2(ks[b] * pp + kv[b] * tt)
                    if k == 0:
                        y[b] = r
                        lost = 1.0 - behind
                    else:
                        y[b] = y[b] + before[b] * (r - last[b])
                        lost = before[b] - behind
                    big[b, k, rows, :] = y[b] + (lost * (r * (r + 1.0))) * (table[2, b] * inv2)
                    before[b] = behind
                    last[b] = r
            for b in range(NB):
                lit[e, pl.ds(ROWS * b + r8, 8), :] = (y[b] - before[b] * last[b]) * table[0, b]

    def make_fronts():
        for p in others():
            sums(p, p).wait_recv()

        @pl.loop(0, ROWS // 8)
        def _(j):
            rows = pl.ds(pl.multiple_of(8 * j, 8), 8)
            for h in range(2):
                part = [sum_r[s, h, rows, :] for s in range(SLABS)]
                for s in range(SLABS):
                    fro_s[s, h, rows, :] = sum(
                        front[a][s] * part[a] for a in range(SLABS) if a != s
                    )

        fro_r[d] = fro_s[d]
        for p in others():
            fronts(p, d).start()

    def same(i):
        return lax.rem(d + 2 * i, SLABS)

    def sax(to, slot):
        return rdma(
            seed_a.at[slot], seed_a.at[slot], sax_ss.at[to // 2], sax_rs.at[slot // 2], {"depth": to}
        )

    def sap(slot):
        return rdma(
            seed_a.at[slot], seed_a.at[slot], sap_ss.at[slot // 2], sap_rs.at[slot // 2], {"depth": pair}
        )

    def spread_seeds():
        @pl.loop(1, COLS)
        def _(o):
            p = lax.rem(w + o, COLS)
            seed_copy(p, p).wait_recv()

        seed_own.wait()
        for b in range(NB):
            for r in range(2):
                for h in range(2):
                    seed_a[d, pl.ds(ROWS * b + r + 16 * h, 8, stride=2), :] = seed_l[
                        pl.ds(8 * h, 8), b, r, :
                    ]
        for i in (2, 1, 3):
            sax(same(i), d).start()
        sap(d).start()

    def forward_seeds():
        for i in (1, 3, 2):
            sax(same(i), same(i)).wait_recv()
            sap(same(i)).start()

    def dims(e, r8):
        pp = fro_r[e, 0, pl.ds(r8, 8), :]
        tt = fro_r[e, 1, pl.ds(r8, 8), :]
        return [jnp.exp2(ks[b] * pp + kv[b] * tt) for b in range(NB)]

    def fade(g0, g1):
        @pl.loop(g0, g1)
        def _(g):
            e, _ = tile_of(4 * g)
            for j in range(4):
                dim = dims(e, 8 * j)
                for b in range(NB):
                    rows = pl.ds(ROWS * b + 8 * j, 8)
                    lit[e, rows, :] = lit[e, rows, :] * dim[b]

    def pairs(i, slot):
        return rdma(
            lit.at[2 * chip(i) + 1 - c],
            pair_r.at[slot],
            pair_ss.at[i],
            pair_rs.at[slot],
            {"depth": pair},
        )

    def chips(i, slot):
        return rdma(
            chip_s.at[i], chip_r.at[slot], chip_ss.at[i], chip_rs.at[slot], {"depth": same(i + 1)}
        )

    def join(i):
        pairs(i, chip(i)).wait_recv()
        e = 2 * chip(i) + c

        @pl.loop(0, 4)
        def _(j):
            rows = pl.ds(pl.multiple_of(64 * j, 64), 64)
            chip_s[i, rows, :] = lit[e, rows, :] + pair_r[chip(i), rows, :]

    heavy(0, 4)
    pl.semaphore_wait(barrier, SLABS + COLS - 2)
    for p in others():
        sums(p, d).start()

    @pl.loop(1, COLS)
    def _(o):
        seed_copy(lax.rem(w + o, COLS), w).start()

    heavy(4, 16)
    make_fronts()
    spread_seeds()
    heavy(16, 32)
    for p in others():
        fronts(p, p).wait_recv()
    for i in range(CHIPS):
        fade(2 * i, 2 * i + 2)
        pairs(i, chip(i)).start()
    for i in range(3):
        join(i)
        chips(i, x).start()
    forward_seeds()
    for s in range(CHIPS):
        sap(2 * s + 1 - c).wait_recv()

    @pl.loop(0, SLABS)
    def _(e):
        for j in range(4):
            total = gas[0] * (seed_a[e, pl.ds(8 * j, 8), :] * lit[e, pl.ds(8 * j, 8), :])
            for b in range(1, NB):
                rows = pl.ds(ROWS * b + 8 * j, 8)
                total = total + gas[b] * (seed_a[e, rows, :] * lit[e, rows, :])
            gs_s[e, pl.ds(8 * j, 8), :] = total

    gs_r[d] = gs_s[d]
    for p in others():
        grads(p, d).start()

    def out_copy(g):
        e, _ = tile_of(4 * g)
        rows = pl.ds(pl.multiple_of(ROWS * e, ROWS), ROWS)
        return pltpu.make_async_copy(
            grad_v.at[:, rows, :], grad_hbm.at[:, rows, :], out_sem.at[g]
        )

    def finish(g0, g1):
        @pl.loop(g0, g1)
        def _(g):
            @pl.loop(0, 4)
            def _(j):
                e, r8 = tile_of(4 * g + j)
                rows = pl.ds(pl.multiple_of(ROWS * e + r8, 8), 8)
                dim = dims(e, r8)
                wt = [
                    table[1, b] * (seed_a[e, pl.ds(ROWS * b + r8, 8), :] * dim[b])
                    for b in range(NB)
                ]
                for k in range(CD):
                    acc = wt[0] * big[0, k, rows, :]
                    for b in range(1, NB):
                        acc = acc + wt[b] * big[b, k, rows, :]
                    grad_v[k, rows, :] = acc

            out_copy(g).start()

    finish(0, SLABS)

    pairs(3, x).wait_recv()
    for i in range(3):
        chips(i, chip(i)).wait_recv()

    @pl.loop(0, 4)
    def _(j):
        rows = pl.ds(pl.multiple_of(64 * j, 64), 64)
        rad_v[rows, :] = (
            (lit[d, rows, :] + pair_r[x, rows, :])
            + (chip_r[chip(0), rows, :] + chip_r[chip(1), rows, :])
            + chip_r[chip(2), rows, :]
        )

    for b in range(NB):
        for r in range(2):
            for h in range(2):
                rad_s[pl.ds(8 * h, 8), b, r, :] = rad_v[
                    pl.ds(ROWS * b + r + 16 * h, 8, stride=2), :
                ]
    rad_r[:, :, cols(w)] = rad_s[w]

    def rad_copy(to, slot):
        return rdma(
            rad_s.at[to], rad_r.at[:, :, cols(slot)], rad_ss.at[to], rad_rs.at[slot], {"width": to}
        )

    @pl.loop(1, COLS)
    def _(o):
        rad_copy(lax.rem(w + o, COLS), w).start()

    for p in others():
        grads(p, p).wait_recv()

    @pl.loop(0, ROWS // 8)
    def _(j):
        rows = pl.ds(pl.multiple_of(8 * j, 8), 8)
        part = [gs_r[s, rows, :] for s in range(SLABS)]
        for s in range(SLABS):
            rest = part[s]
            for a in range(SLABS):
                if a != s:
                    rest = rest + front[s][a] * part[a]
            q_s[s, rows, :] = rest

    q_r[d] = q_s[d]
    for p in others():
        quots(p, d).start()

    for p in others():
        quots(p, p).wait_recv()
    q_out[...] = q_r[...]

    @pl.loop(1, COLS)
    def _(o):
        p = lax.rem(w + o, COLS)
        rad_copy(p, p).wait_recv()

    rad_out[...] = rad_r[...]
    for g in range(SLABS):
        out_copy(g).wait()
    for p in others():
        sums(p, d).wait_send()
        fronts(p, d).wait_send()
        grads(p, d).wait_send()
        quots(p, d).wait_send()
    for i in (1, 2, 3):
        sax(same(i), d).wait_send()
    for s in range(CHIPS):
        sap(2 * s + c).wait_send()
        pairs(s, chip(s)).wait_send()
    for i in range(3):
        chips(i, x).wait_send()

    @pl.loop(1, COLS)
    def _(o):
        p = lax.rem(w + o, COLS)
        seed_copy(p, w).wait_send()
        rad_copy(p, w).wait_send()


def subtract_kernel(g_ref, q_ref, o_ref):
    q = q_ref[...]
    for k in range(CD):
        o_ref[k] = g_ref[k] - q


def on_device(
    thermal_field,
    particulate_fraction,
    sootiness_extinction,
    vapour_extinction_rate,
    planck_over_wavelength,
    layer_sightline_position,
    picture_adjoint_seed,
):
    smem = pl.BlockSpec(memory_space=pltpu.SMEM)
    vmem = pl.BlockSpec(memory_space=pltpu.VMEM)
    hbm = pl.BlockSpec(memory_space=pl.ANY)

    def v(*shape):
        return pltpu.VMEM(shape, F32)

    def sems(*shape):
        return pltpu.SemaphoreType.DMA(shape)

    field = (CD, LINES, LANES)
    image = (NB * ROWS, LANES)
    radiance, gradient, quot = pl.pallas_call(
        kernel,
        out_shape=(
            jax.ShapeDtypeStruct((NB, 2, COLS * LANES), F32),
            jax.ShapeDtypeStruct(field, F32),
            jax.ShapeDtypeStruct((SLABS, ROWS, LANES), F32),
        ),
        in_specs=[smem, smem, smem, smem, hbm, hbm, hbm],
        out_specs=(vmem, hbm, vmem),
        scratch_shapes=[
            v(*field),
            pltpu.VMEM(field, jnp.bfloat16),
            v(*field),
            v(NB, *field),
            v(3, NB, *TILE),
            v(SLABS, 2, ROWS, LANES),
            v(SLABS, 2, ROWS, LANES),
            v(SLABS, 2, ROWS, LANES),
            v(SLABS, 2, ROWS, LANES),
            v(COLS, NB, 2, LANES),
            v(SLABS, *image),
            v(SLABS, *image),
            v(CHIPS, *image),
            v(3, *image),
            v(CHIPS, *image),
            v(SLABS, ROWS, LANES),
            v(SLABS, ROWS, LANES),
            v(SLABS, ROWS, LANES),
            v(SLABS, ROWS, LANES),
            v(*image),
            v(COLS, NB, 2, LANES),
            v(NB, 2, COLS * LANES),
            v(*field),
            sems(2, CHIPS),
            sems(SLABS + 1),
            sems(SLABS),
            sems(SLABS),
            sems(SLABS),
            sems(SLABS),
            sems(COLS),
            sems(COLS),
            sems(CHIPS),
            sems(CHIPS),
            sems(CHIPS),
            sems(CHIPS),
            sems(CHIPS),
            sems(CHIPS),
            sems(3),
            sems(CHIPS),
            sems(SLABS),
            sems(SLABS),
            sems(SLABS),
            sems(SLABS),
            sems(COLS),
            sems(COLS),
        ],
        compiler_params=pltpu.CompilerParams(
            collective_id=0, has_side_effects=True, vmem_limit_bytes=56 << 20
        ),
    )(
        sootiness_extinction,
        vapour_extinction_rate,
        planck_over_wavelength,
        layer_sightline_position,
        thermal_field,
        particulate_fraction,
        picture_adjoint_seed,
    )
    cells = pl.BlockSpec((CD, 2 * ROWS, LANES), lambda i: (0, i, 0))
    gradient = pl.pallas_call(
        subtract_kernel,
        grid=(LINES // (2 * ROWS),),
        out_shape=jax.ShapeDtypeStruct(field, F32),
        in_specs=[cells, pl.BlockSpec((2 * ROWS, LANES), lambda i: (i, 0))],
        out_specs=cells,
    )(gradient, quot.reshape(LINES, LANES))
    return radiance, gradient


def solution(mesh):
    placed = (
        P("depth", None, "width"),
        P("depth", None, "width"),
        P(),
        P(),
        P(),
        P(),
        P(None, ("depth", "width"), None),
    )
    return jax.shard_map(
        on_device,
        mesh=mesh,
        in_specs=placed,
        out_specs=(P(None, ("depth", "width"), None), P("depth", None, "width")),
        check_vma=False,
    )
```

```python
import math

import jax
import jax.numpy as jnp
from jax import lax
from jax.experimental import pallas as pl
from jax.experimental.pallas import tpu as pltpu
from jax.sharding import PartitionSpec as P

MESH = pl.DeviceIdType.MESH
NB = 8
CD = 16
SLABS = 8
COLS = 16
CHIPS = 4
LINES = 256
ROWS = 32
LANES = 128
TILE = (8, LANES)
LOG2E = math.log2(math.e)
F32 = jnp.float32


def kernel(
    soot,
    vapour,
    planck,
    pos,
    t_hbm,
    p_hbm,
    seed_hbm,
    rad_out,
    grad_v,
    q_out,
    t_v,
    p_v,
    pf,
    big,
    table,
    sum_s,
    sum_r,
    fro_s,
    fro_r,
    seed_l,
    seed_a,
    lit,
    pair_r,
    chip_s,
    chip_r,
    gs_s,
    gs_r,
    q_s,
    q_r,
    rad_v,
    rad_s,
    rad_r,
    in_sem,
    out_sem,
    sum_ss,
    sum_rs,
    fro_ss,
    fro_rs,
    seed_ss,
    seed_rs,
    sax_ss,
    sax_rs,
    sap_ss,
    sap_rs,
    pair_ss,
    pair_rs,
    chip_ss,
    chip_rs,
    gs_ss,
    gs_rs,
    q_ss,
    q_rs,
    rad_ss,
    rad_rs,
):
    d = lax.axis_index("depth")
    w = lax.axis_index("width")
    c = lax.rem(d, 2)
    x = d // 2
    pair = d + 1 - 2 * c

    def chip(i):
        return lax.rem(x + 1 + i, CHIPS)

    def tile_of(n):
        g = n // 4
        e = 2 * chip(g // 2) + lax.rem(g + 1 + c, 2)
        return e, pl.multiple_of(8 * lax.rem(n, 4), 8)

    def rdma(src, dst, ss, rs, dev):
        return pltpu.make_async_remote_copy(
            src_ref=src, dst_ref=dst, send_sem=ss, recv_sem=rs, device_id=dev, device_id_type=MESH
        )

    def loads(i):
        rows = pl.ds(pl.multiple_of(64 * chip(i), 64), 64)
        return (
            pltpu.make_async_copy(t_hbm.at[:, rows, :], t_v.at[:, rows, :], in_sem.at[0, i]),
            pltpu.make_async_copy(p_hbm.at[:, rows, :], p_v.at[:, rows, :], in_sem.at[1, i]),
        )

    for i in range(CHIPS):
        for cp in loads(i):
            cp.start()

    barrier = pltpu.get_barrier_semaphore()
    for o in range(1, SLABS):
        pl.semaphore_signal(
            barrier, inc=1, device_id={"depth": lax.rem(d + o, SLABS)}, device_id_type=MESH
        )
    for o in range(1, COLS):
        pl.semaphore_signal(
            barrier, inc=1, device_id={"width": lax.rem(w + o, COLS)}, device_id_type=MESH
        )

    ks = [soot[b] * (-LOG2E / CD) for b in range(NB)]
    kv = [vapour[b] * (-LOG2E / CD) for b in range(NB)]
    kp = [planck[b] * LOG2E for b in range(NB)]
    gas = [vapour[b] * (1.0 / CD) for b in range(NB)]
    front = [
        [jnp.where(pos[i] < pos[j], 1.0, 0.0) for j in range(SLABS)] for i in range(SLABS)
    ]
    for b in range(NB):
        scale = jnp.exp(jnp.full(TILE, 0.5 * planck[b], F32)) - 1.0
        table[0, b] = scale
        table[1, b] = scale * gas[b]
        table[2, b] = jnp.full(TILE, planck[b], F32) / gas[b]

    def cols(i):
        return pl.ds(pl.multiple_of(i * LANES, LANES), LANES)

    def seed_copy(to, slot):
        return rdma(
            seed_hbm.at[:, :, cols(to)], seed_l.at[slot], seed_ss.at[to], seed_rs.at[slot], {"width": to}
        )

    seed_own = pltpu.make_async_copy(seed_hbm.at[:, :, cols(w)], seed_l.at[w], out_sem.at[SLABS])
    seed_own.start()
    pl.semaphore_wait(barrier, SLABS + COLS - 2)

    @pl.loop(1, COLS)
    def _(o):
        seed_copy(lax.rem(w + o, COLS), w).start()

    def exchange(send, recv, ss, rs):
        def make(to, slot):
            return rdma(send.at[to], recv.at[slot], ss.at[to], rs.at[slot], {"depth": to})

        return make

    sums = exchange(sum_s, sum_r, sum_ss, sum_rs)
    fronts = exchange(fro_s, fro_r, fro_ss, fro_rs)
    grads = exchange(gs_s, gs_r, gs_ss, gs_rs)
    quots = exchange(q_s, q_r, q_ss, q_rs)

    def others():
        return [lax.rem(d + o, SLABS) for o in (2, 3, 4, 5, 6, 7, 1)]

    for i in range(CHIPS):
        for cp in loads(i):
            cp.wait()
        for half in range(2):
            e = 2 * chip(i) + lax.rem(half + 1 + c, 2)

            @pl.loop(0, 2)
            def _(j):
                r16 = pl.multiple_of(16 * j, 16)
                rows = pl.ds(pl.multiple_of(ROWS * e + r16, 16), 16)
                pp = jnp.zeros((16, LANES), F32)
                tt = jnp.zeros((16, LANES), F32)
                for k in range(CD):
                    p = p_v[k, rows, :].astype(F32)
                    pf[k, rows, :] = p
                    pp = pp + p
                    tt = tt + t_v[k, rows, :]
                if i == CHIPS - 1 and half == 1:
                    sum_r[d, 0, pl.ds(r16, 16), :] = pp
                    sum_r[d, 1, pl.ds(r16, 16), :] = tt
                else:
                    sum_s[e, 0, pl.ds(r16, 16), :] = pp
                    sum_s[e, 1, pl.ds(r16, 16), :] = tt

            if not (i == CHIPS - 1 and half == 1):
                sums(e, d).start()


    def heavy(n0, n1):
        @pl.loop(n0, n1)
        def _(n):
            e, r8 = tile_of(n)
            rows = pl.ds(pl.multiple_of(ROWS * e + r8, 8), 8)
            pp = jnp.zeros(TILE, F32)
            tt = jnp.zeros(TILE, F32)
            before = [None] * NB
            y = [None] * NB
            last = [None] * NB
            for k in range(CD):
                t = t_v[k, rows, :]
                pp = pp + pf[k, rows, :]
                tt = tt + t
                inv = 1.0 / t
                inv2 = inv * inv
                for b in range(NB):
                    r = 1.0 / (jnp.exp2(kp[b] * inv) - 1.0)
                    behind = jnp.exp2(ks[b] * pp + kv[b] * tt)
                    if k == 0:
                        y[b] = r
                        lost = 1.0 - behind
                    else:
                        y[b] = y[b] + before[b] * (r - last[b])
                        lost = before[b] - behind
                    big[b, k, rows, :] = y[b] + (lost * (r * (r + 1.0))) * (table[2, b] * inv2)
                    before[b] = behind
                    last[b] = r
            for b in range(NB):
                lit[e, pl.ds(ROWS * b + r8, 8), :] = (y[b] - before[b] * last[b]) * table[0, b]

    def make_fronts():
        for p in others():
            sums(p, p).wait_recv()

        @pl.loop(0, ROWS // 8)
        def _(j):
            rows = pl.ds(pl.multiple_of(8 * j, 8), 8)
            for h in range(2):
                part = [sum_r[s, h, rows, :] for s in range(SLABS)]
                for s in range(SLABS):
                    fro_s[s, h, rows, :] = sum(
                        front[a][s] * part[a] for a in range(SLABS) if a != s
                    )

        fro_r[d] = fro_s[d]
        for p in others():
            fronts(p, d).start()

    def same(i):
        return lax.rem(d + 2 * i, SLABS)

    def sax(to, slot):
        return rdma(
            seed_a.at[slot], seed_a.at[slot], sax_ss.at[to // 2], sax_rs.at[slot // 2], {"depth": to}
        )

    def sap(slot):
        return rdma(
            seed_a.at[slot], seed_a.at[slot], sap_ss.at[slot // 2], sap_rs.at[slot // 2], {"depth": pair}
        )

    def spread_seeds():
        @pl.loop(1, COLS)
        def _(o):
            p = lax.rem(w + o, COLS)
            seed_copy(p, p).wait_recv()

        seed_own.wait()
        for b in range(NB):
            for r in range(2):
                for h in range(2):
                    seed_a[d, pl.ds(ROWS * b + r + 16 * h, 8, stride=2), :] = seed_l[
                        pl.ds(8 * h, 8), b, r, :
                    ]
        for i in (2, 1, 3):
            sax(same(i), d).start()
        sap(d).start()

    def forward_seeds():
        for i in (1, 3, 2):
            sax(same(i), same(i)).wait_recv()
            sap(same(i)).start()

    def dims(e, r8):
        pp = fro_r[e, 0, pl.ds(r8, 8), :]
        tt = fro_r[e, 1, pl.ds(r8, 8), :]
        return [jnp.exp2(ks[b] * pp + kv[b] * tt) for b in range(NB)]

    def fade(g0, g1):
        @pl.loop(g0, g1)
        def _(g):
            e, _ = tile_of(4 * g)
            for j in range(4):
                dim = dims(e, 8 * j)
                for b in range(NB):
                    rows = pl.ds(ROWS * b + 8 * j, 8)
                    lit[e, rows, :] = lit[e, rows, :] * dim[b]

    def pairs(i, slot):
        return rdma(
            lit.at[2 * chip(i) + 1 - c],
            pair_r.at[slot],
            pair_ss.at[i],
            pair_rs.at[slot],
            {"depth": pair},
        )

    def chips(i, slot):
        return rdma(
            chip_s.at[i], chip_r.at[slot], chip_ss.at[i], chip_rs.at[slot], {"depth": same(i + 1)}
        )

    def join(i):
        pairs(i, chip(i)).wait_recv()
        e = 2 * chip(i) + c

        @pl.loop(0, 4)
        def _(j):
            rows = pl.ds(pl.multiple_of(64 * j, 64), 64)
            chip_s[i, rows, :] = lit[e, rows, :] + pair_r[chip(i), rows, :]

    heavy(0, 12)
    make_fronts()
    heavy(12, 20)
    spread_seeds()
    heavy(20, 24)
    for p in others():
        fronts(p, p).wait_recv()
    for i in range(3):
        fade(2 * i, 2 * i + 2)
        pairs(i, chip(i)).start()
    heavy(24, 28)
    fade(6, 7)
    pairs(3, chip(3)).start()
    for i in range(3):
        join(i)
        chips(i, x).start()
    heavy(28, 32)
    fade(7, 8)
    forward_seeds()
    for s in range(CHIPS):
        sap(2 * s + 1 - c).wait_recv()

    @pl.loop(0, SLABS)
    def _(e):
        for j in range(4):
            total = gas[0] * (seed_a[e, pl.ds(8 * j, 8), :] * lit[e, pl.ds(8 * j, 8), :])
            for b in range(1, NB):
                rows = pl.ds(ROWS * b + 8 * j, 8)
                total = total + gas[b] * (seed_a[e, rows, :] * lit[e, rows, :])
            gs_s[e, pl.ds(8 * j, 8), :] = total

    gs_r[d] = gs_s[d]
    for p in others():
        grads(p, d).start()

    def finish(g0, g1):
        @pl.loop(g0, g1)
        def _(g):
            @pl.loop(0, 4)
            def _(j):
                e, r8 = tile_of(4 * g + j)
                rows = pl.ds(pl.multiple_of(ROWS * e + r8, 8), 8)
                dim = dims(e, r8)
                wt = [
                    table[1, b] * (seed_a[e, pl.ds(ROWS * b + r8, 8), :] * dim[b])
                    for b in range(NB)
                ]
                for k in range(CD):
                    acc = wt[0] * big[0, k, rows, :]
                    for b in range(1, NB):
                        acc = acc + wt[b] * big[b, k, rows, :]
                    grad_v[k, rows, :] = acc


    finish(0, SLABS)

    pairs(3, x).wait_recv()
    for i in range(3):
        chips(i, chip(i)).wait_recv()

    @pl.loop(0, 4)
    def _(j):
        rows = pl.ds(pl.multiple_of(64 * j, 64), 64)
        rad_v[rows, :] = (
            (lit[d, rows, :] + pair_r[x, rows, :])
            + (chip_r[chip(0), rows, :] + chip_r[chip(1), rows, :])
            + chip_r[chip(2), rows, :]
        )

    for b in range(NB):
        for r in range(2):
            for h in range(2):
                rad_s[pl.ds(8 * h, 8), b, r, :] = rad_v[
                    pl.ds(ROWS * b + r + 16 * h, 8, stride=2), :
                ]
    rad_r[:, :, cols(w)] = rad_s[w]

    def rad_copy(to, slot):
        return rdma(
            rad_s.at[to], rad_r.at[:, :, cols(slot)], rad_ss.at[to], rad_rs.at[slot], {"width": to}
        )

    @pl.loop(1, COLS)
    def _(o):
        rad_copy(lax.rem(w + o, COLS), w).start()

    for p in others():
        grads(p, p).wait_recv()

    @pl.loop(0, ROWS // 8)
    def _(j):
        rows = pl.ds(pl.multiple_of(8 * j, 8), 8)
        part = [gs_r[s, rows, :] for s in range(SLABS)]
        for s in range(SLABS):
            rest = part[s]
            for a in range(SLABS):
                if a != s:
                    rest = rest + front[s][a] * part[a]
            q_s[s, rows, :] = rest

    q_r[d] = q_s[d]
    for p in others():
        quots(p, d).start()

    for p in others():
        quots(p, p).wait_recv()
    q_out[...] = q_r[...]

    @pl.loop(1, COLS)
    def _(o):
        p = lax.rem(w + o, COLS)
        rad_copy(p, p).wait_recv()

    rad_out[...] = rad_r[...]
    for p in others():
        sums(p, d).wait_send()
        fronts(p, d).wait_send()
        grads(p, d).wait_send()
        quots(p, d).wait_send()
    for i in (1, 2, 3):
        sax(same(i), d).wait_send()
    for s in range(CHIPS):
        sap(2 * s + c).wait_send()
        pairs(s, chip(s)).wait_send()
    for i in range(3):
        chips(i, x).wait_send()

    @pl.loop(1, COLS)
    def _(o):
        p = lax.rem(w + o, COLS)
        seed_copy(p, w).wait_send()
        rad_copy(p, w).wait_send()


def subtract_kernel(q_ref, g_ref, r_ref, o_hbm, rad_hbm, buf, out_sem):
    picture = pltpu.make_async_copy(r_ref, rad_hbm, out_sem.at[CD])
    picture.start()

    def store(k):
        return pltpu.make_async_copy(buf.at[k], o_hbm.at[k], out_sem.at[k])

    for k in range(CD):
        for e in range(SLABS):
            rows = pl.ds(ROWS * e, ROWS)
            buf[k, rows, :] = g_ref[k, rows, :] - q_ref[e]
        store(k).start()
    for k in range(CD):
        store(k).wait()
    picture.wait()


def on_device(
    thermal_field,
    particulate_fraction,
    sootiness_extinction,
    vapour_extinction_rate,
    planck_over_wavelength,
    layer_sightline_position,
    picture_adjoint_seed,
):
    smem = pl.BlockSpec(memory_space=pltpu.SMEM)
    vmem = pl.BlockSpec(memory_space=pltpu.VMEM)
    hbm = pl.BlockSpec(memory_space=pl.ANY)

    def v(*shape):
        return pltpu.VMEM(shape, F32)

    def sems(*shape):
        return pltpu.SemaphoreType.DMA(shape)

    field = (CD, LINES, LANES)
    image = (NB * ROWS, LANES)
    radiance, gradient, quot = pl.pallas_call(
        kernel,
        out_shape=(
            pltpu.VMEM((NB, 2, COLS * LANES), F32),
            pltpu.VMEM(field, F32),
            pltpu.VMEM((SLABS, ROWS, LANES), F32),
        ),
        in_specs=[smem, smem, smem, smem, hbm, hbm, hbm],
        out_specs=(vmem, vmem, vmem),
        scratch_shapes=[
            v(*field),
            pltpu.VMEM(field, jnp.bfloat16),
            v(*field),
            v(NB, *field),
            v(3, NB, *TILE),
            v(SLABS, 2, ROWS, LANES),
            v(SLABS, 2, ROWS, LANES),
            v(SLABS, 2, ROWS, LANES),
            v(SLABS, 2, ROWS, LANES),
            v(COLS, NB, 2, LANES),
            v(SLABS, *image),
            v(SLABS, *image),
            v(CHIPS, *image),
            v(3, *image),
            v(CHIPS, *image),
            v(SLABS, ROWS, LANES),
            v(SLABS, ROWS, LANES),
            v(SLABS, ROWS, LANES),
            v(SLABS, ROWS, LANES),
            v(*image),
            v(COLS, NB, 2, LANES),
            v(NB, 2, COLS * LANES),
            sems(2, CHIPS),
            sems(SLABS + 1),
            sems(SLABS),
            sems(SLABS),
            sems(SLABS),
            sems(SLABS),
            sems(COLS),
            sems(COLS),
            sems(CHIPS),
            sems(CHIPS),
            sems(CHIPS),
            sems(CHIPS),
            sems(CHIPS),
            sems(CHIPS),
            sems(3),
            sems(CHIPS),
            sems(SLABS),
            sems(SLABS),
            sems(SLABS),
            sems(SLABS),
            sems(COLS),
            sems(COLS),
        ],
        compiler_params=pltpu.CompilerParams(
            collective_id=0, has_side_effects=True, vmem_limit_bytes=56 << 20
        ),
    )(
        sootiness_extinction,
        vapour_extinction_rate,
        planck_over_wavelength,
        layer_sightline_position,
        thermal_field,
        particulate_fraction,
        picture_adjoint_seed,
    )
    gradient, radiance = pl.pallas_call(
        subtract_kernel,
        out_shape=(
            jax.ShapeDtypeStruct(field, F32),
            jax.ShapeDtypeStruct((NB, 2, COLS * LANES), F32),
        ),
        in_specs=[vmem, vmem, vmem],
        out_specs=(hbm, hbm),
        scratch_shapes=[v(*field), sems(CD + 1)],
        compiler_params=pltpu.CompilerParams(vmem_limit_bytes=8 << 20),
    )(quot, gradient, radiance)
    return radiance, gradient


def solution(mesh):
    placed = (
        P("depth", None, "width"),
        P("depth", None, "width"),
        P(),
        P(),
        P(),
        P(),
        P(None, ("depth", "width"), None),
    )
    return jax.shard_map(
        on_device,
        mesh=mesh,
        in_specs=placed,
        out_specs=(P(None, ("depth", "width"), None), P("depth", None, "width")),
        check_vma=False,
    )
```

```python
import math

import jax
import jax.numpy as jnp
from jax import lax
from jax.experimental import pallas as pl
from jax.experimental.pallas import tpu as pltpu
from jax.sharding import PartitionSpec as P

MESH = pl.DeviceIdType.MESH
NB = 8
CD = 16
SLABS = 8
COLS = 16
CHIPS = 4
LINES = 256
ROWS = 32
LANES = 128
TILE = (8, LANES)
LOG2E = math.log2(math.e)
F32 = jnp.float32


def kernel(
    soot,
    vapour,
    planck,
    pos,
    t_hbm,
    p_hbm,
    seed_hbm,
    rad_out,
    grad_v,
    q_out,
    t_v,
    p_v,
    pf,
    big,
    table,
    sum_s,
    sum_r,
    fro_s,
    fro_r,
    seed_l,
    seed_a,
    lit,
    pair_r,
    chip_s,
    chip_r,
    gs_s,
    gs_r,
    q_s,
    q_r,
    rad_v,
    rad_s,
    rad_r,
    in_sem,
    out_sem,
    sum_ss,
    sum_rs,
    fro_ss,
    fro_rs,
    seed_ss,
    seed_rs,
    sax_ss,
    sax_rs,
    sap_ss,
    sap_rs,
    pair_ss,
    pair_rs,
    chip_ss,
    chip_rs,
    gs_ss,
    gs_rs,
    q_ss,
    q_rs,
    rad_ss,
    rad_rs,
):
    d = lax.axis_index("depth")
    w = lax.axis_index("width")
    c = lax.rem(d, 2)
    x = d // 2
    pair = d + 1 - 2 * c

    def chip(i):
        return lax.rem(x + 1 + i, CHIPS)

    def tile_of(n):
        g = n // 4
        e = 2 * chip(g // 2) + lax.rem(g + 1 + c, 2)
        return e, pl.multiple_of(8 * lax.rem(n, 4), 8)

    def rdma(src, dst, ss, rs, dev):
        return pltpu.make_async_remote_copy(
            src_ref=src, dst_ref=dst, send_sem=ss, recv_sem=rs, device_id=dev, device_id_type=MESH
        )

    def loads(i):
        rows = pl.ds(pl.multiple_of(64 * chip(i), 64), 64)
        return (
            pltpu.make_async_copy(t_hbm.at[:, rows, :], t_v.at[:, rows, :], in_sem.at[0, i]),
            pltpu.make_async_copy(p_hbm.at[:, rows, :], p_v.at[:, rows, :], in_sem.at[1, i]),
        )

    for i in range(CHIPS):
        for cp in loads(i):
            cp.start()

    barrier = pltpu.get_barrier_semaphore()
    for o in range(1, SLABS):
        pl.semaphore_signal(
            barrier, inc=1, device_id={"depth": lax.rem(d + o, SLABS)}, device_id_type=MESH
        )
    for o in range(1, COLS):
        pl.semaphore_signal(
            barrier, inc=1, device_id={"width": lax.rem(w + o, COLS)}, device_id_type=MESH
        )

    ks = [soot[b] * (-LOG2E / CD) for b in range(NB)]
    kv = [vapour[b] * (-LOG2E / CD) for b in range(NB)]
    kp = [planck[b] * LOG2E for b in range(NB)]
    gas = [vapour[b] * (1.0 / CD) for b in range(NB)]
    front = [
        [jnp.where(pos[i] < pos[j], 1.0, 0.0) for j in range(SLABS)] for i in range(SLABS)
    ]
    for b in range(NB):
        scale = jnp.exp(jnp.full(TILE, 0.5 * planck[b], F32)) - 1.0
        table[0, b] = scale
        table[1, b] = scale * gas[b]
        table[2, b] = jnp.full(TILE, planck[b], F32) / gas[b]

    def cols(i):
        return pl.ds(pl.multiple_of(i * LANES, LANES), LANES)

    def seed_copy(to, slot):
        return rdma(
            seed_hbm.at[:, :, cols(to)], seed_l.at[slot], seed_ss.at[to], seed_rs.at[slot], {"width": to}
        )

    seed_own = pltpu.make_async_copy(seed_hbm.at[:, :, cols(w)], seed_l.at[w], out_sem.at[SLABS])
    seed_own.start()
    pl.semaphore_wait(barrier, SLABS + COLS - 2)

    @pl.loop(1, COLS)
    def _(o):
        seed_copy(lax.rem(w + o, COLS), w).start()

    def exchange(send, recv, ss, rs):
        def make(to, slot):
            return rdma(send.at[to], recv.at[slot], ss.at[to], rs.at[slot], {"depth": to})

        return make

    sums = exchange(sum_s, sum_r, sum_ss, sum_rs)
    fronts = exchange(fro_s, fro_r, fro_ss, fro_rs)
    grads = exchange(gs_s, gs_r, gs_ss, gs_rs)
    quots = exchange(q_s, q_r, q_ss, q_rs)

    def others():
        return [lax.rem(d + o, SLABS) for o in (2, 3, 4, 5, 6, 7, 1)]

    for i in range(CHIPS):
        for cp in loads(i):
            cp.wait()
        for half in range(2):
            e = 2 * chip(i) + lax.rem(half + 1 + c, 2)

            @pl.loop(0, 2)
            def _(j):
                r16 = pl.multiple_of(16 * j, 16)
                rows = pl.ds(pl.multiple_of(ROWS * e + r16, 16), 16)
                pp = jnp.zeros((16, LANES), F32)
                tt = jnp.zeros((16, LANES), F32)
                for k in range(CD):
                    p = p_v[k, rows, :].astype(F32)
                    pf[k, rows, :] = p
                    pp = pp + p
                    tt = tt + t_v[k, rows, :]
                if i == CHIPS - 1 and half == 1:
                    sum_r[d, 0, pl.ds(r16, 16), :] = pp
                    sum_r[d, 1, pl.ds(r16, 16), :] = tt
                else:
                    sum_s[e, 0, pl.ds(r16, 16), :] = pp
                    sum_s[e, 1, pl.ds(r16, 16), :] = tt

            if not (i == CHIPS - 1 and half == 1):
                sums(e, d).start()


    def heavy(n0, n1):
        @pl.loop(n0, n1)
        def _(n):
            e, r8 = tile_of(n)
            rows = pl.ds(pl.multiple_of(ROWS * e + r8, 8), 8)
            pp = jnp.zeros(TILE, F32)
            tt = jnp.zeros(TILE, F32)
            before = [None] * NB
            y = [None] * NB
            last = [None] * NB
            for k in range(CD):
                t = t_v[k, rows, :]
                pp = pp + pf[k, rows, :]
                tt = tt + t
                inv = 1.0 / t
                inv2 = inv * inv
                for b in range(NB):
                    r = 1.0 / (jnp.exp2(kp[b] * inv) - 1.0)
                    behind = jnp.exp2(ks[b] * pp + kv[b] * tt)
                    if k == 0:
                        y[b] = r
                        lost = 1.0 - behind
                    else:
                        y[b] = y[b] + before[b] * (r - last[b])
                        lost = before[b] - behind
                    big[b, k, rows, :] = y[b] + (lost * (r * (r + 1.0))) * (table[2, b] * inv2)
                    before[b] = behind
                    last[b] = r
            for b in range(NB):
                lit[e, pl.ds(ROWS * b + r8, 8), :] = (y[b] - before[b] * last[b]) * table[0, b]

    def make_fronts():
        for p in others():
            sums(p, p).wait_recv()

        @pl.loop(0, ROWS // 8)
        def _(j):
            rows = pl.ds(pl.multiple_of(8 * j, 8), 8)
            for h in range(2):
                part = [sum_r[s, h, rows, :] for s in range(SLABS)]
                for s in range(SLABS):
                    fro_s[s, h, rows, :] = sum(
                        front[a][s] * part[a] for a in range(SLABS) if a != s
                    )

        fro_r[d] = fro_s[d]
        for p in others():
            fronts(p, d).start()

    def same(i):
        return lax.rem(d + 2 * i, SLABS)

    def sax(to, slot):
        return rdma(
            seed_a.at[slot], seed_a.at[slot], sax_ss.at[to // 2], sax_rs.at[slot // 2], {"depth": to}
        )

    def sap(slot):
        return rdma(
            seed_a.at[slot], seed_a.at[slot], sap_ss.at[slot // 2], sap_rs.at[slot // 2], {"depth": pair}
        )

    def spread_seeds():
        @pl.loop(1, COLS)
        def _(o):
            p = lax.rem(w + o, COLS)
            seed_copy(p, p).wait_recv()

        seed_own.wait()
        for b in range(NB):
            for r in range(2):
                for h in range(2):
                    seed_a[d, pl.ds(ROWS * b + r + 16 * h, 8, stride=2), :] = seed_l[
                        pl.ds(8 * h, 8), b, r, :
                    ]
        for i in (2, 1, 3):
            sax(same(i), d).start()
        sap(d).start()

    def forward_seeds():
        for i in (1, 3, 2):
            sax(same(i), same(i)).wait_recv()
            sap(same(i)).start()

    def dims(e, r8):
        pp = fro_r[e, 0, pl.ds(r8, 8), :]
        tt = fro_r[e, 1, pl.ds(r8, 8), :]
        return [jnp.exp2(ks[b] * pp + kv[b] * tt) for b in range(NB)]

    def fade(g0, g1):
        @pl.loop(g0, g1)
        def _(g):
            e, _ = tile_of(4 * g)
            for j in range(4):
                dim = dims(e, 8 * j)
                for b in range(NB):
                    rows = pl.ds(ROWS * b + 8 * j, 8)
                    lit[e, rows, :] = lit[e, rows, :] * dim[b]

    def pairs(i, slot):
        return rdma(
            lit.at[2 * chip(i) + 1 - c],
            pair_r.at[slot],
            pair_ss.at[i],
            pair_rs.at[slot],
            {"depth": pair},
        )

    def chips(i, slot):
        return rdma(
            chip_s.at[i], chip_r.at[slot], chip_ss.at[i], chip_rs.at[slot], {"depth": same(i + 1)}
        )

    def join(i):
        pairs(i, chip(i)).wait_recv()
        e = 2 * chip(i) + c

        @pl.loop(0, 4)
        def _(j):
            rows = pl.ds(pl.multiple_of(64 * j, 64), 64)
            chip_s[i, rows, :] = lit[e, rows, :] + pair_r[chip(i), rows, :]

    heavy(0, 12)
    make_fronts()
    heavy(12, 16)
    spread_seeds()
    heavy(16, 24)
    for p in others():
        fronts(p, p).wait_recv()
    for i in range(3):
        fade(2 * i, 2 * i + 2)
        pairs(i, chip(i)).start()
    heavy(24, 26)
    for i in range(3):
        join(i)
        chips(i, x).start()
    heavy(26, 32)
    fade(6, 8)
    pairs(3, chip(3)).start()
    forward_seeds()
    for s in range(CHIPS):
        sap(2 * s + 1 - c).wait_recv()

    @pl.loop(0, SLABS)
    def _(e):
        for j in range(4):
            total = gas[0] * (seed_a[e, pl.ds(8 * j, 8), :] * lit[e, pl.ds(8 * j, 8), :])
            for b in range(1, NB):
                rows = pl.ds(ROWS * b + 8 * j, 8)
                total = total + gas[b] * (seed_a[e, rows, :] * lit[e, rows, :])
            gs_s[e, pl.ds(8 * j, 8), :] = total

    gs_r[d] = gs_s[d]
    for p in others():
        grads(p, d).start()

    def finish(g0, g1):
        @pl.loop(g0, g1)
        def _(g):
            @pl.loop(0, 4)
            def _(j):
                e, r8 = tile_of(4 * g + j)
                rows = pl.ds(pl.multiple_of(ROWS * e + r8, 8), 8)
                dim = dims(e, r8)
                wt = [
                    table[1, b] * (seed_a[e, pl.ds(ROWS * b + r8, 8), :] * dim[b])
                    for b in range(NB)
                ]
                for k in range(CD):
                    acc = wt[0] * big[0, k, rows, :]
                    for b in range(1, NB):
                        acc = acc + wt[b] * big[b, k, rows, :]
                    grad_v[k, rows, :] = acc


    finish(0, SLABS)

    pairs(3, x).wait_recv()
    for i in range(3):
        chips(i, chip(i)).wait_recv()

    @pl.loop(0, 4)
    def _(j):
        rows = pl.ds(pl.multiple_of(64 * j, 64), 64)
        rad_v[rows, :] = (
            (lit[d, rows, :] + pair_r[x, rows, :])
            + (chip_r[chip(0), rows, :] + chip_r[chip(1), rows, :])
            + chip_r[chip(2), rows, :]
        )

    for b in range(NB):
        for r in range(2):
            for h in range(2):
                rad_s[pl.ds(8 * h, 8), b, r, :] = rad_v[
                    pl.ds(ROWS * b + r + 16 * h, 8, stride=2), :
                ]
    rad_r[:, :, cols(w)] = rad_s[w]

    def rad_copy(to, slot):
        return rdma(
            rad_s.at[to], rad_r.at[:, :, cols(slot)], rad_ss.at[to], rad_rs.at[slot], {"width": to}
        )

    @pl.loop(1, COLS)
    def _(o):
        rad_copy(lax.rem(w + o, COLS), w).start()

    for p in others():
        grads(p, p).wait_recv()

    @pl.loop(0, ROWS // 8)
    def _(j):
        rows = pl.ds(pl.multiple_of(8 * j, 8), 8)
        part = [gs_r[s, rows, :] for s in range(SLABS)]
        for s in range(SLABS):
            rest = part[s]
            for a in range(SLABS):
                if a != s:
                    rest = rest + front[s][a] * part[a]
            q_s[s, rows, :] = rest

    q_r[d] = q_s[d]
    for p in others():
        quots(p, d).start()

    for p in others():
        quots(p, p).wait_recv()
    q_out[...] = q_r[...]

    @pl.loop(1, COLS)
    def _(o):
        p = lax.rem(w + o, COLS)
        rad_copy(p, p).wait_recv()

    rad_out[...] = rad_r[...]
    for p in others():
        sums(p, d).wait_send()
        fronts(p, d).wait_send()
        grads(p, d).wait_send()
        quots(p, d).wait_send()
    for i in (1, 2, 3):
        sax(same(i), d).wait_send()
    for s in range(CHIPS):
        sap(2 * s + c).wait_send()
        pairs(s, chip(s)).wait_send()
    for i in range(3):
        chips(i, x).wait_send()

    @pl.loop(1, COLS)
    def _(o):
        p = lax.rem(w + o, COLS)
        seed_copy(p, w).wait_send()
        rad_copy(p, w).wait_send()


def subtract_kernel(q_ref, g_ref, r_ref, o_hbm, rad_hbm, buf, out_sem):
    picture = pltpu.make_async_copy(r_ref, rad_hbm, out_sem.at[CD])
    picture.start()

    def store(k):
        return pltpu.make_async_copy(buf.at[k], o_hbm.at[k], out_sem.at[k])

    for k in range(CD):
        for e in range(SLABS):
            rows = pl.ds(ROWS * e, ROWS)
            buf[k, rows, :] = g_ref[k, rows, :] - q_ref[e]
        store(k).start()
    for k in range(CD):
        store(k).wait()
    picture.wait()


def on_device(
    thermal_field,
    particulate_fraction,
    sootiness_extinction,
    vapour_extinction_rate,
    planck_over_wavelength,
    layer_sightline_position,
    picture_adjoint_seed,
):
    smem = pl.BlockSpec(memory_space=pltpu.SMEM)
    vmem = pl.BlockSpec(memory_space=pltpu.VMEM)
    hbm = pl.BlockSpec(memory_space=pl.ANY)

    def v(*shape):
        return pltpu.VMEM(shape, F32)

    def sems(*shape):
        return pltpu.SemaphoreType.DMA(shape)

    field = (CD, LINES, LANES)
    image = (NB * ROWS, LANES)
    radiance, gradient, quot = pl.pallas_call(
        kernel,
        out_shape=(
            pltpu.VMEM((NB, 2, COLS * LANES), F32),
            pltpu.VMEM(field, F32),
            pltpu.VMEM((SLABS, ROWS, LANES), F32),
        ),
        in_specs=[smem, smem, smem, smem, hbm, hbm, hbm],
        out_specs=(vmem, vmem, vmem),
        scratch_shapes=[
            v(*field),
            pltpu.VMEM(field, jnp.bfloat16),
            v(*field),
            v(NB, *field),
            v(3, NB, *TILE),
            v(SLABS, 2, ROWS, LANES),
            v(SLABS, 2, ROWS, LANES),
            v(SLABS, 2, ROWS, LANES),
            v(SLABS, 2, ROWS, LANES),
            v(COLS, NB, 2, LANES),
            v(SLABS, *image),
            v(SLABS, *image),
            v(CHIPS, *image),
            v(3, *image),
            v(CHIPS, *image),
            v(SLABS, ROWS, LANES),
            v(SLABS, ROWS, LANES),
            v(SLABS, ROWS, LANES),
            v(SLABS, ROWS, LANES),
            v(*image),
            v(COLS, NB, 2, LANES),
            v(NB, 2, COLS * LANES),
            sems(2, CHIPS),
            sems(SLABS + 1),
            sems(SLABS),
            sems(SLABS),
            sems(SLABS),
            sems(SLABS),
            sems(COLS),
            sems(COLS),
            sems(CHIPS),
            sems(CHIPS),
            sems(CHIPS),
            sems(CHIPS),
            sems(CHIPS),
            sems(CHIPS),
            sems(3),
            sems(CHIPS),
            sems(SLABS),
            sems(SLABS),
            sems(SLABS),
            sems(SLABS),
            sems(COLS),
            sems(COLS),
        ],
        compiler_params=pltpu.CompilerParams(
            collective_id=0, has_side_effects=True, vmem_limit_bytes=56 << 20
        ),
    )(
        sootiness_extinction,
        vapour_extinction_rate,
        planck_over_wavelength,
        layer_sightline_position,
        thermal_field,
        particulate_fraction,
        picture_adjoint_seed,
    )
    gradient, radiance = pl.pallas_call(
        subtract_kernel,
        out_shape=(
            jax.ShapeDtypeStruct(field, F32),
            jax.ShapeDtypeStruct((NB, 2, COLS * LANES), F32),
        ),
        in_specs=[vmem, vmem, vmem],
        out_specs=(hbm, hbm),
        scratch_shapes=[v(*field), sems(CD + 1)],
        compiler_params=pltpu.CompilerParams(vmem_limit_bytes=8 << 20),
    )(quot, gradient, radiance)
    return radiance, gradient


def solution(mesh):
    placed = (
        P("depth", None, "width"),
        P("depth", None, "width"),
        P(),
        P(),
        P(),
        P(),
        P(None, ("depth", "width"), None),
    )
    return jax.shard_map(
        on_device,
        mesh=mesh,
        in_specs=placed,
        out_specs=(P(None, ("depth", "width"), None), P("depth", None, "width")),
        check_vma=False,
    )
```

```python
import math

import jax
import jax.numpy as jnp
from jax import lax
from jax.experimental import pallas as pl
from jax.experimental.pallas import tpu as pltpu
from jax.sharding import PartitionSpec as P

MESH = pl.DeviceIdType.MESH
NB = 8
CD = 16
SLABS = 8
COLS = 16
CHIPS = 4
LINES = 256
ROWS = 32
LANES = 128
TILE = (8, LANES)
LOG2E = math.log2(math.e)
F32 = jnp.float32


def kernel(
    soot,
    vapour,
    planck,
    pos,
    t_hbm,
    p_hbm,
    seed_hbm,
    rad_out,
    grad_v,
    q_out,
    t_v,
    p_v,
    pf,
    big,
    table,
    sum_s,
    sum_r,
    fro_s,
    fro_r,
    seed_l,
    seed_a,
    lit,
    pair_r,
    chip_s,
    chip_r,
    gs_s,
    gs_r,
    q_s,
    q_r,
    rad_v,
    rad_s,
    rad_r,
    in_sem,
    out_sem,
    sum_ss,
    sum_rs,
    fro_ss,
    fro_rs,
    seed_ss,
    seed_rs,
    sax_ss,
    sax_rs,
    sap_ss,
    sap_rs,
    pair_ss,
    pair_rs,
    chip_ss,
    chip_rs,
    gs_ss,
    gs_rs,
    q_ss,
    q_rs,
    rad_ss,
    rad_rs,
):
    d = lax.axis_index("depth")
    w = lax.axis_index("width")
    c = lax.rem(d, 2)
    x = d // 2
    pair = d + 1 - 2 * c

    def chip(i):
        return lax.rem(x + 1 + i, CHIPS)

    def tile_of(n):
        g = n // 4
        e = 2 * chip(g // 2) + lax.rem(g + 1 + c, 2)
        return e, pl.multiple_of(8 * lax.rem(n, 4), 8)

    def rdma(src, dst, ss, rs, dev):
        return pltpu.make_async_remote_copy(
            src_ref=src, dst_ref=dst, send_sem=ss, recv_sem=rs, device_id=dev, device_id_type=MESH
        )

    def loads(i):
        rows = pl.ds(pl.multiple_of(64 * chip(i), 64), 64)
        return (
            pltpu.make_async_copy(t_hbm.at[:, rows, :], t_v.at[:, rows, :], in_sem.at[0, i]),
            pltpu.make_async_copy(p_hbm.at[:, rows, :], p_v.at[:, rows, :], in_sem.at[1, i]),
        )

    for i in range(CHIPS):
        for cp in loads(i):
            cp.start()

    barrier = pltpu.get_barrier_semaphore()
    for o in range(1, SLABS):
        pl.semaphore_signal(
            barrier, inc=1, device_id={"depth": lax.rem(d + o, SLABS)}, device_id_type=MESH
        )
    for o in range(1, COLS):
        pl.semaphore_signal(
            barrier, inc=1, device_id={"width": lax.rem(w + o, COLS)}, device_id_type=MESH
        )

    ks = [soot[b] * (-LOG2E / CD) for b in range(NB)]
    kv = [vapour[b] * (-LOG2E / CD) for b in range(NB)]
    kp = [planck[b] * LOG2E for b in range(NB)]
    gas = [vapour[b] * (1.0 / CD) for b in range(NB)]
    front = [
        [jnp.where(pos[i] < pos[j], 1.0, 0.0) for j in range(SLABS)] for i in range(SLABS)
    ]
    for b in range(NB):
        scale = jnp.exp(jnp.full(TILE, 0.5 * planck[b], F32)) - 1.0
        table[0, b] = scale
        table[1, b] = scale * gas[b]
        table[2, b] = jnp.full(TILE, planck[b], F32) / gas[b]

    def cols(i):
        return pl.ds(pl.multiple_of(i * LANES, LANES), LANES)

    def seed_copy(to, slot):
        return rdma(
            seed_hbm.at[:, :, cols(to)], seed_l.at[slot], seed_ss.at[to], seed_rs.at[slot], {"width": to}
        )

    seed_own = pltpu.make_async_copy(seed_hbm.at[:, :, cols(w)], seed_l.at[w], out_sem.at[SLABS])
    seed_own.start()
    pl.semaphore_wait(barrier, SLABS + COLS - 2)

    steps = sorted(
        ((a, b) for a in range(4) for b in range(4) if a or b),
        key=lambda s: -(min(s[0], 4 - s[0]) + min(s[1], 4 - s[1])),
    )
    across = [4 * lax.rem(w // 4 + a, 4) + lax.rem(lax.rem(w, 4) + b, 4) for a, b in steps]
    for p in across:
        seed_copy(p, w).start()

    def exchange(send, recv, ss, rs):
        def make(to, slot):
            return rdma(send.at[to], recv.at[slot], ss.at[to], rs.at[slot], {"depth": to})

        return make

    sums = exchange(sum_s, sum_r, sum_ss, sum_rs)
    fronts = exchange(fro_s, fro_r, fro_ss, fro_rs)
    grads = exchange(gs_s, gs_r, gs_ss, gs_rs)
    quots = exchange(q_s, q_r, q_ss, q_rs)

    def others():
        return [lax.rem(d + o, SLABS) for o in (2, 3, 4, 5, 6, 7, 1)]

    for i in range(CHIPS):
        for cp in loads(i):
            cp.wait()
        for half in range(2):
            e = 2 * chip(i) + lax.rem(half + 1 + c, 2)

            @pl.loop(0, 2)
            def _(j):
                r16 = pl.multiple_of(16 * j, 16)
                rows = pl.ds(pl.multiple_of(ROWS * e + r16, 16), 16)
                pp = jnp.zeros((16, LANES), F32)
                tt = jnp.zeros((16, LANES), F32)
                for k in range(CD):
                    p = p_v[k, rows, :].astype(F32)
                    pf[k, rows, :] = p
                    pp = pp + p
                    tt = tt + t_v[k, rows, :]
                if i == CHIPS - 1 and half == 1:
                    sum_r[d, 0, pl.ds(r16, 16), :] = pp
                    sum_r[d, 1, pl.ds(r16, 16), :] = tt
                else:
                    sum_s[e, 0, pl.ds(r16, 16), :] = pp
                    sum_s[e, 1, pl.ds(r16, 16), :] = tt

            if not (i == CHIPS - 1 and half == 1):
                sums(e, d).start()


    def heavy(n0, n1):
        @pl.loop(n0, n1)
        def _(n):
            e, r8 = tile_of(n)
            rows = pl.ds(pl.multiple_of(ROWS * e + r8, 8), 8)
            pp = jnp.zeros(TILE, F32)
            tt = jnp.zeros(TILE, F32)
            before = [None] * NB
            y = [None] * NB
            last = [None] * NB
            for k in range(CD):
                t = t_v[k, rows, :]
                pp = pp + pf[k, rows, :]
                tt = tt + t
                inv = 1.0 / t
                inv2 = inv * inv
                for b in range(NB):
                    r = 1.0 / (jnp.exp2(kp[b] * inv) - 1.0)
                    behind = jnp.exp2(ks[b] * pp + kv[b] * tt)
                    if k == 0:
                        y[b] = r
                        lost = 1.0 - behind
                    else:
                        y[b] = y[b] + before[b] * (r - last[b])
                        lost = before[b] - behind
                    big[b, k, rows, :] = y[b] + (lost * (r * (r + 1.0))) * (table[2, b] * inv2)
                    before[b] = behind
                    last[b] = r
            for b in range(NB):
                lit[e, pl.ds(ROWS * b + r8, 8), :] = (y[b] - before[b] * last[b]) * table[0, b]

    def make_fronts():
        for p in others():
            sums(p, p).wait_recv()

        @pl.loop(0, ROWS // 8)
        def _(j):
            rows = pl.ds(pl.multiple_of(8 * j, 8), 8)
            for h in range(2):
                part = [sum_r[s, h, rows, :] for s in range(SLABS)]
                for s in range(SLABS):
                    fro_s[s, h, rows, :] = sum(
                        front[a][s] * part[a] for a in range(SLABS) if a != s
                    )

        fro_r[d] = fro_s[d]
        for p in others():
            fronts(p, d).start()

    def same(i):
        return lax.rem(d + 2 * i, SLABS)

    def sax(to, slot):
        return rdma(
            seed_a.at[slot], seed_a.at[slot], sax_ss.at[to // 2], sax_rs.at[slot // 2], {"depth": to}
        )

    def sap(slot):
        return rdma(
            seed_a.at[slot], seed_a.at[slot], sap_ss.at[slot // 2], sap_rs.at[slot // 2], {"depth": pair}
        )

    def spread_seeds():
        @pl.loop(1, COLS)
        def _(o):
            p = lax.rem(w + o, COLS)
            seed_copy(p, p).wait_recv()

        seed_own.wait()
        for b in range(NB):
            for r in range(2):
                for h in range(2):
                    seed_a[d, pl.ds(ROWS * b + r + 16 * h, 8, stride=2), :] = seed_l[
                        pl.ds(8 * h, 8), b, r, :
                    ]
        for i in (2, 1, 3):
            sax(same(i), d).start()
        sap(d).start()

    def forward_seeds():
        for i in (1, 3, 2):
            sax(same(i), same(i)).wait_recv()
            sap(same(i)).start()

    def dims(e, r8):
        pp = fro_r[e, 0, pl.ds(r8, 8), :]
        tt = fro_r[e, 1, pl.ds(r8, 8), :]
        return [jnp.exp2(ks[b] * pp + kv[b] * tt) for b in range(NB)]

    def fade(g0, g1):
        @pl.loop(g0, g1)
        def _(g):
            e, _ = tile_of(4 * g)
            for j in range(4):
                dim = dims(e, 8 * j)
                for b in range(NB):
                    rows = pl.ds(ROWS * b + 8 * j, 8)
                    lit[e, rows, :] = lit[e, rows, :] * dim[b]

    def pairs(i, slot):
        return rdma(
            lit.at[2 * chip(i) + 1 - c],
            pair_r.at[slot],
            pair_ss.at[i],
            pair_rs.at[slot],
            {"depth": pair},
        )

    def chips(i, slot):
        return rdma(
            chip_s.at[i], chip_r.at[slot], chip_ss.at[i], chip_rs.at[slot], {"depth": same(i + 1)}
        )

    def join(i):
        pairs(i, chip(i)).wait_recv()
        e = 2 * chip(i) + c

        @pl.loop(0, 4)
        def _(j):
            rows = pl.ds(pl.multiple_of(64 * j, 64), 64)
            chip_s[i, rows, :] = lit[e, rows, :] + pair_r[chip(i), rows, :]

    heavy(0, 12)
    make_fronts()
    heavy(12, 16)
    spread_seeds()
    heavy(16, 24)
    for p in others():
        fronts(p, p).wait_recv()
    for i in range(3):
        fade(2 * i, 2 * i + 2)
        pairs(i, chip(i)).start()
    heavy(24, 26)
    for i in range(3):
        join(i)
        chips(i, x).start()
    heavy(26, 32)
    fade(6, 8)
    pairs(3, chip(3)).start()
    forward_seeds()
    for s in range(CHIPS):
        sap(2 * s + 1 - c).wait_recv()

    @pl.loop(0, SLABS)
    def _(e):
        for j in range(4):
            total = gas[0] * (seed_a[e, pl.ds(8 * j, 8), :] * lit[e, pl.ds(8 * j, 8), :])
            for b in range(1, NB):
                rows = pl.ds(ROWS * b + 8 * j, 8)
                total = total + gas[b] * (seed_a[e, rows, :] * lit[e, rows, :])
            gs_s[e, pl.ds(8 * j, 8), :] = total

    gs_r[d] = gs_s[d]
    for p in others():
        grads(p, d).start()

    def finish(g0, g1):
        @pl.loop(g0, g1)
        def _(g):
            @pl.loop(0, 4)
            def _(j):
                e, r8 = tile_of(4 * g + j)
                rows = pl.ds(pl.multiple_of(ROWS * e + r8, 8), 8)
                dim = dims(e, r8)
                wt = [
                    table[1, b] * (seed_a[e, pl.ds(ROWS * b + r8, 8), :] * dim[b])
                    for b in range(NB)
                ]
                for k in range(CD):
                    acc = wt[0] * big[0, k, rows, :]
                    for b in range(1, NB):
                        acc = acc + wt[b] * big[b, k, rows, :]
                    grad_v[k, rows, :] = acc


    finish(0, SLABS)

    pairs(3, x).wait_recv()
    for i in range(3):
        chips(i, chip(i)).wait_recv()

    @pl.loop(0, 4)
    def _(j):
        rows = pl.ds(pl.multiple_of(64 * j, 64), 64)
        rad_v[rows, :] = (
            (lit[d, rows, :] + pair_r[x, rows, :])
            + (chip_r[chip(0), rows, :] + chip_r[chip(1), rows, :])
            + chip_r[chip(2), rows, :]
        )

    for b in range(NB):
        for r in range(2):
            for h in range(2):
                rad_s[pl.ds(8 * h, 8), b, r, :] = rad_v[
                    pl.ds(ROWS * b + r + 16 * h, 8, stride=2), :
                ]
    rad_r[:, :, cols(w)] = rad_s[w]

    def rad_copy(to, slot):
        return rdma(
            rad_s.at[to], rad_r.at[:, :, cols(slot)], rad_ss.at[to], rad_rs.at[slot], {"width": to}
        )

    for p in across:
        rad_copy(p, w).start()

    for p in others():
        grads(p, p).wait_recv()

    @pl.loop(0, ROWS // 8)
    def _(j):
        rows = pl.ds(pl.multiple_of(8 * j, 8), 8)
        part = [gs_r[s, rows, :] for s in range(SLABS)]
        for s in range(SLABS):
            rest = part[s]
            for a in range(SLABS):
                if a != s:
                    rest = rest + front[s][a] * part[a]
            q_s[s, rows, :] = rest

    q_r[d] = q_s[d]
    for p in others():
        quots(p, d).start()

    for p in others():
        quots(p, p).wait_recv()
    q_out[...] = q_r[...]

    @pl.loop(1, COLS)
    def _(o):
        p = lax.rem(w + o, COLS)
        rad_copy(p, p).wait_recv()

    rad_out[...] = rad_r[...]
    for p in others():
        sums(p, d).wait_send()
        fronts(p, d).wait_send()
        grads(p, d).wait_send()
        quots(p, d).wait_send()
    for i in (1, 2, 3):
        sax(same(i), d).wait_send()
    for s in range(CHIPS):
        sap(2 * s + c).wait_send()
        pairs(s, chip(s)).wait_send()
    for i in range(3):
        chips(i, x).wait_send()

    @pl.loop(1, COLS)
    def _(o):
        p = lax.rem(w + o, COLS)
        seed_copy(p, w).wait_send()
        rad_copy(p, w).wait_send()


def subtract_kernel(q_ref, g_ref, r_ref, o_hbm, rad_hbm, buf, out_sem):
    picture = pltpu.make_async_copy(r_ref, rad_hbm, out_sem.at[CD])
    picture.start()

    def store(k):
        return pltpu.make_async_copy(buf.at[k], o_hbm.at[k], out_sem.at[k])

    for k in range(CD):
        for e in range(SLABS):
            rows = pl.ds(ROWS * e, ROWS)
            buf[k, rows, :] = g_ref[k, rows, :] - q_ref[e]
        store(k).start()
    for k in range(CD):
        store(k).wait()
    picture.wait()


def on_device(
    thermal_field,
    particulate_fraction,
    sootiness_extinction,
    vapour_extinction_rate,
    planck_over_wavelength,
    layer_sightline_position,
    picture_adjoint_seed,
):
    smem = pl.BlockSpec(memory_space=pltpu.SMEM)
    vmem = pl.BlockSpec(memory_space=pltpu.VMEM)
    hbm = pl.BlockSpec(memory_space=pl.ANY)

    def v(*shape):
        return pltpu.VMEM(shape, F32)

    def sems(*shape):
        return pltpu.SemaphoreType.DMA(shape)

    field = (CD, LINES, LANES)
    image = (NB * ROWS, LANES)
    radiance, gradient, quot = pl.pallas_call(
        kernel,
        out_shape=(
            pltpu.VMEM((NB, 2, COLS * LANES), F32),
            pltpu.VMEM(field, F32),
            pltpu.VMEM((SLABS, ROWS, LANES), F32),
        ),
        in_specs=[smem, smem, smem, smem, hbm, hbm, hbm],
        out_specs=(vmem, vmem, vmem),
        scratch_shapes=[
            v(*field),
            pltpu.VMEM(field, jnp.bfloat16),
            v(*field),
            v(NB, *field),
            v(3, NB, *TILE),
            v(SLABS, 2, ROWS, LANES),
            v(SLABS, 2, ROWS, LANES),
            v(SLABS, 2, ROWS, LANES),
            v(SLABS, 2, ROWS, LANES),
            v(COLS, NB, 2, LANES),
            v(SLABS, *image),
            v(SLABS, *image),
            v(CHIPS, *image),
            v(3, *image),
            v(CHIPS, *image),
            v(SLABS, ROWS, LANES),
            v(SLABS, ROWS, LANES),
            v(SLABS, ROWS, LANES),
            v(SLABS, ROWS, LANES),
            v(*image),
            v(COLS, NB, 2, LANES),
            v(NB, 2, COLS * LANES),
            sems(2, CHIPS),
            sems(SLABS + 1),
            sems(SLABS),
            sems(SLABS),
            sems(SLABS),
            sems(SLABS),
            sems(COLS),
            sems(COLS),
            sems(CHIPS),
            sems(CHIPS),
            sems(CHIPS),
            sems(CHIPS),
            sems(CHIPS),
            sems(CHIPS),
            sems(3),
            sems(CHIPS),
            sems(SLABS),
            sems(SLABS),
            sems(SLABS),
            sems(SLABS),
            sems(COLS),
            sems(COLS),
        ],
        compiler_params=pltpu.CompilerParams(
            collective_id=0, has_side_effects=True, vmem_limit_bytes=56 << 20
        ),
    )(
        sootiness_extinction,
        vapour_extinction_rate,
        planck_over_wavelength,
        layer_sightline_position,
        thermal_field,
        particulate_fraction,
        picture_adjoint_seed,
    )
    gradient, radiance = pl.pallas_call(
        subtract_kernel,
        out_shape=(
            jax.ShapeDtypeStruct(field, F32),
            jax.ShapeDtypeStruct((NB, 2, COLS * LANES), F32),
        ),
        in_specs=[vmem, vmem, vmem],
        out_specs=(hbm, hbm),
        scratch_shapes=[v(*field), sems(CD + 1)],
        compiler_params=pltpu.CompilerParams(vmem_limit_bytes=8 << 20),
    )(quot, gradient, radiance)
    return radiance, gradient


def solution(mesh):
    placed = (
        P("depth", None, "width"),
        P("depth", None, "width"),
        P(),
        P(),
        P(),
        P(),
        P(None, ("depth", "width"), None),
    )
    return jax.shard_map(
        on_device,
        mesh=mesh,
        in_specs=placed,
        out_specs=(P(None, ("depth", "width"), None), P("depth", None, "width")),
        check_vma=False,
    )
```

```python
import math

import jax
import jax.numpy as jnp
from jax import lax
from jax.experimental import pallas as pl
from jax.experimental.pallas import tpu as pltpu
from jax.sharding import PartitionSpec as P

MESH = pl.DeviceIdType.MESH
NB = 8
CD = 16
SLABS = 8
COLS = 16
CHIPS = 4
LINES = 256
ROWS = 32
LANES = 128
TILE = (8, LANES)
LOG2E = math.log2(math.e)
F32 = jnp.float32


def kernel(
    soot,
    vapour,
    planck,
    pos,
    t_hbm,
    p_hbm,
    seed_hbm,
    rad_out,
    grad_v,
    q_out,
    t_v,
    p_v,
    pf,
    big,
    table,
    sum_s,
    sum_r,
    fro_s,
    fro_r,
    seed_l,
    seed_a,
    lit,
    pair_r,
    chip_s,
    chip_r,
    gs_s,
    gs_r,
    q_s,
    q_r,
    rad_v,
    rad_s,
    rad_r,
    in_sem,
    out_sem,
    sum_ss,
    sum_rs,
    fro_ss,
    fro_rs,
    seed_ss,
    seed_rs,
    sax_ss,
    sax_rs,
    sap_ss,
    sap_rs,
    pair_ss,
    pair_rs,
    chip_ss,
    chip_rs,
    gs_ss,
    gs_rs,
    q_ss,
    q_rs,
    rad_ss,
    rad_rs,
):
    d = lax.axis_index("depth")
    w = lax.axis_index("width")
    c = lax.rem(d, 2)
    x = d // 2
    pair = d + 1 - 2 * c

    def chip(i):
        return lax.rem(x + 1 + i, CHIPS)

    def tile_of(n):
        g = n // 4
        e = 2 * chip(g // 2) + lax.rem(g + 1 + c, 2)
        return e, pl.multiple_of(8 * lax.rem(n, 4), 8)

    def rdma(src, dst, ss, rs, dev):
        return pltpu.make_async_remote_copy(
            src_ref=src, dst_ref=dst, send_sem=ss, recv_sem=rs, device_id=dev, device_id_type=MESH
        )

    def loads(i):
        rows = pl.ds(pl.multiple_of(64 * chip(i), 64), 64)
        return (
            pltpu.make_async_copy(t_hbm.at[:, rows, :], t_v.at[:, rows, :], in_sem.at[0, i]),
            pltpu.make_async_copy(p_hbm.at[:, rows, :], p_v.at[:, rows, :], in_sem.at[1, i]),
        )

    for i in range(CHIPS):
        for cp in loads(i):
            cp.start()

    barrier = pltpu.get_barrier_semaphore()
    for o in range(1, SLABS):
        pl.semaphore_signal(
            barrier, inc=1, device_id={"depth": lax.rem(d + o, SLABS)}, device_id_type=MESH
        )
    for o in range(1, COLS):
        pl.semaphore_signal(
            barrier, inc=1, device_id={"width": lax.rem(w + o, COLS)}, device_id_type=MESH
        )

    ks = [soot[b] * (-LOG2E / CD) for b in range(NB)]
    kv = [vapour[b] * (-LOG2E / CD) for b in range(NB)]
    kp = [planck[b] * LOG2E for b in range(NB)]
    gas = [vapour[b] * (1.0 / CD) for b in range(NB)]
    front = [
        [jnp.where(pos[i] < pos[j], 1.0, 0.0) for j in range(SLABS)] for i in range(SLABS)
    ]
    for b in range(NB):
        scale = jnp.exp(jnp.full(TILE, 0.5 * planck[b], F32)) - 1.0
        table[0, b] = scale
        table[1, b] = scale * gas[b]
        table[2, b] = jnp.full(TILE, planck[b], F32) / gas[b]

    def cols(i):
        return pl.ds(pl.multiple_of(i * LANES, LANES), LANES)

    def seed_copy(to, slot):
        return rdma(
            seed_hbm.at[:, :, cols(to)], seed_l.at[slot], seed_ss.at[to], seed_rs.at[slot], {"width": to}
        )

    seed_own = pltpu.make_async_copy(seed_hbm.at[:, :, cols(w)], seed_l.at[w], out_sem.at[SLABS])
    seed_own.start()
    pl.semaphore_wait(barrier, SLABS + COLS - 2)

    @pl.loop(1, COLS)
    def _(o):
        seed_copy(lax.rem(w + o, COLS), w).start()

    def exchange(send, recv, ss, rs):
        def make(to, slot):
            return rdma(send.at[to], recv.at[slot], ss.at[to], rs.at[slot], {"depth": to})

        return make

    sums = exchange(sum_s, sum_r, sum_ss, sum_rs)
    fronts = exchange(fro_s, fro_r, fro_ss, fro_rs)
    grads = exchange(gs_s, gs_r, gs_ss, gs_rs)
    quots = exchange(q_s, q_r, q_ss, q_rs)

    def others():
        return [lax.rem(d + o, SLABS) for o in (2, 3, 4, 5, 6, 7, 1)]

    for i in range(CHIPS):
        for cp in loads(i):
            cp.wait()
        for half in range(2):
            e = 2 * chip(i) + lax.rem(half + 1 + c, 2)

            @pl.loop(0, 2)
            def _(j):
                r16 = pl.multiple_of(16 * j, 16)
                rows = pl.ds(pl.multiple_of(ROWS * e + r16, 16), 16)
                pp = jnp.zeros((16, LANES), F32)
                tt = jnp.zeros((16, LANES), F32)
                for k in range(CD):
                    p = p_v[k, rows, :].astype(F32)
                    pf[k, rows, :] = p
                    pp = pp + p
                    tt = tt + t_v[k, rows, :]
                if i == CHIPS - 1 and half == 1:
                    sum_r[d, 0, pl.ds(r16, 16), :] = pp
                    sum_r[d, 1, pl.ds(r16, 16), :] = tt
                else:
                    sum_s[e, 0, pl.ds(r16, 16), :] = pp
                    sum_s[e, 1, pl.ds(r16, 16), :] = tt

            if not (i == CHIPS - 1 and half == 1):
                sums(e, d).start()


    def heavy(n0, n1):
        @pl.loop(n0, n1)
        def _(n):
            e, r8 = tile_of(n)
            rows = pl.ds(pl.multiple_of(ROWS * e + r8, 8), 8)
            pp = jnp.zeros(TILE, F32)
            tt = jnp.zeros(TILE, F32)
            before = [None] * NB
            y = [None] * NB
            last = [None] * NB
            for k in range(CD):
                t = t_v[k, rows, :]
                pp = pp + pf[k, rows, :]
                tt = tt + t
                inv = 1.0 / t
                inv2 = inv * inv
                for b in range(NB):
                    r = 1.0 / (jnp.exp2(kp[b] * inv) - 1.0)
                    behind = jnp.exp2(ks[b] * pp + kv[b] * tt)
                    if k == 0:
                        y[b] = r
                        lost = 1.0 - behind
                    else:
                        y[b] = y[b] + before[b] * (r - last[b])
                        lost = before[b] - behind
                    big[b, k, rows, :] = y[b] + (lost * (r * (r + 1.0))) * (table[2, b] * inv2)
                    before[b] = behind
                    last[b] = r
            for b in range(NB):
                lit[e, pl.ds(ROWS * b + r8, 8), :] = (y[b] - before[b] * last[b]) * table[0, b]

    def make_fronts():
        for p in others():
            sums(p, p).wait_recv()

        @pl.loop(0, ROWS // 8)
        def _(j):
            rows = pl.ds(pl.multiple_of(8 * j, 8), 8)
            for h in range(2):
                part = [sum_r[s, h, rows, :] for s in range(SLABS)]
                for s in range(SLABS):
                    fro_s[s, h, rows, :] = sum(
                        front[a][s] * part[a] for a in range(SLABS) if a != s
                    )

        fro_r[d] = fro_s[d]
        for p in others():
            fronts(p, d).start()

    def same(i):
        return lax.rem(d + 2 * i, SLABS)

    def sax(to, slot, h):
        part = seed_a.at[slot, pl.ds(NB * ROWS // 2 * h, NB * ROWS // 2)]
        return rdma(
            part, part, sax_ss.at[2 * (to // 2) + h], sax_rs.at[2 * (slot // 2) + h], {"depth": to}
        )

    def sap(slot, h):
        part = seed_a.at[slot, pl.ds(NB * ROWS // 2 * h, NB * ROWS // 2)]
        return rdma(
            part, part, sap_ss.at[2 * (slot // 2) + h], sap_rs.at[2 * (slot // 2) + h], {"depth": pair}
        )

    def spread_seeds():
        @pl.loop(1, COLS)
        def _(o):
            p = lax.rem(w + o, COLS)
            seed_copy(p, p).wait_recv()

        seed_own.wait()
        for b in range(NB):
            for r in range(2):
                for h in range(2):
                    seed_a[d, pl.ds(ROWS * b + r + 16 * h, 8, stride=2), :] = seed_l[
                        pl.ds(8 * h, 8), b, r, :
                    ]

    def send_seeds(h):
        for i in (2, 1, 3):
            sax(same(i), d, h).start()
        sap(d, h).start()

    def forward_seeds():
        for h in range(2):
            for i in (1, 3, 2):
                sax(same(i), same(i), h).wait_recv()
                sap(same(i), h).start()

    def dims(e, r8):
        pp = fro_r[e, 0, pl.ds(r8, 8), :]
        tt = fro_r[e, 1, pl.ds(r8, 8), :]
        return [jnp.exp2(ks[b] * pp + kv[b] * tt) for b in range(NB)]

    def fade(g0, g1):
        @pl.loop(g0, g1)
        def _(g):
            e, _ = tile_of(4 * g)
            for j in range(4):
                dim = dims(e, 8 * j)
                for b in range(NB):
                    rows = pl.ds(ROWS * b + 8 * j, 8)
                    lit[e, rows, :] = lit[e, rows, :] * dim[b]

    def pairs(i, slot):
        return rdma(
            lit.at[2 * chip(i) + 1 - c],
            pair_r.at[slot],
            pair_ss.at[i],
            pair_rs.at[slot],
            {"depth": pair},
        )

    def chips(i, slot):
        return rdma(
            chip_s.at[i], chip_r.at[slot], chip_ss.at[i], chip_rs.at[slot], {"depth": same(i + 1)}
        )

    def join(i):
        pairs(i, chip(i)).wait_recv()
        e = 2 * chip(i) + c

        @pl.loop(0, 4)
        def _(j):
            rows = pl.ds(pl.multiple_of(64 * j, 64), 64)
            chip_s[i, rows, :] = lit[e, rows, :] + pair_r[chip(i), rows, :]

    heavy(0, 12)
    make_fronts()
    spread_seeds()
    send_seeds(0)
    heavy(12, 20)
    send_seeds(1)
    heavy(20, 24)
    for p in others():
        fronts(p, p).wait_recv()
    for i in range(3):
        fade(2 * i, 2 * i + 2)
        pairs(i, chip(i)).start()
    heavy(24, 28)
    fade(6, 7)
    pairs(3, chip(3)).start()
    for i in range(3):
        join(i)
        chips(i, x).start()
    heavy(28, 32)
    fade(7, 8)
    forward_seeds()
    for s in range(CHIPS):
        for h in range(2):
            sap(2 * s + 1 - c, h).wait_recv()

    @pl.loop(0, SLABS)
    def _(e):
        for j in range(4):
            total = gas[0] * (seed_a[e, pl.ds(8 * j, 8), :] * lit[e, pl.ds(8 * j, 8), :])
            for b in range(1, NB):
                rows = pl.ds(ROWS * b + 8 * j, 8)
                total = total + gas[b] * (seed_a[e, rows, :] * lit[e, rows, :])
            gs_s[e, pl.ds(8 * j, 8), :] = total

    gs_r[d] = gs_s[d]
    for p in others():
        grads(p, d).start()

    def finish(g0, g1):
        @pl.loop(g0, g1)
        def _(g):
            @pl.loop(0, 4)
            def _(j):
                e, r8 = tile_of(4 * g + j)
                rows = pl.ds(pl.multiple_of(ROWS * e + r8, 8), 8)
                dim = dims(e, r8)
                wt = [
                    table[1, b] * (seed_a[e, pl.ds(ROWS * b + r8, 8), :] * dim[b])
                    for b in range(NB)
                ]
                for k in range(CD):
                    acc = wt[0] * big[0, k, rows, :]
                    for b in range(1, NB):
                        acc = acc + wt[b] * big[b, k, rows, :]
                    grad_v[k, rows, :] = acc


    finish(0, SLABS)

    pairs(3, x).wait_recv()
    for i in range(3):
        chips(i, chip(i)).wait_recv()

    @pl.loop(0, 4)
    def _(j):
        rows = pl.ds(pl.multiple_of(64 * j, 64), 64)
        rad_v[rows, :] = (
            (lit[d, rows, :] + pair_r[x, rows, :])
            + (chip_r[chip(0), rows, :] + chip_r[chip(1), rows, :])
            + chip_r[chip(2), rows, :]
        )

    for b in range(NB):
        for r in range(2):
            for h in range(2):
                rad_s[pl.ds(8 * h, 8), b, r, :] = rad_v[
                    pl.ds(ROWS * b + r + 16 * h, 8, stride=2), :
                ]
    rad_r[:, :, cols(w)] = rad_s[w]

    def rad_copy(to, slot):
        return rdma(
            rad_s.at[to], rad_r.at[:, :, cols(slot)], rad_ss.at[to], rad_rs.at[slot], {"width": to}
        )

    @pl.loop(1, COLS)
    def _(o):
        rad_copy(lax.rem(w + o, COLS), w).start()

    for p in others():
        grads(p, p).wait_recv()

    @pl.loop(0, ROWS // 8)
    def _(j):
        rows = pl.ds(pl.multiple_of(8 * j, 8), 8)
        part = [gs_r[s, rows, :] for s in range(SLABS)]
        for s in range(SLABS):
            rest = part[s]
            for a in range(SLABS):
                if a != s:
                    rest = rest + front[s][a] * part[a]
            q_s[s, rows, :] = rest

    q_r[d] = q_s[d]
    for p in others():
        quots(p, d).start()

    for p in others():
        quots(p, p).wait_recv()
    q_out[...] = q_r[...]

    @pl.loop(1, COLS)
    def _(o):
        p = lax.rem(w + o, COLS)
        rad_copy(p, p).wait_recv()

    rad_out[...] = rad_r[...]
    for p in others():
        sums(p, d).wait_send()
        fronts(p, d).wait_send()
        grads(p, d).wait_send()
        quots(p, d).wait_send()
    for i in (1, 2, 3):
        for h in range(2):
            sax(same(i), d, h).wait_send()
    for s in range(CHIPS):
        for h in range(2):
            sap(2 * s + c, h).wait_send()
        pairs(s, chip(s)).wait_send()
    for i in range(3):
        chips(i, x).wait_send()

    @pl.loop(1, COLS)
    def _(o):
        p = lax.rem(w + o, COLS)
        seed_copy(p, w).wait_send()
        rad_copy(p, w).wait_send()


def subtract_kernel(q_ref, g_ref, r_ref, o_hbm, rad_hbm, buf, out_sem):
    picture = pltpu.make_async_copy(r_ref, rad_hbm, out_sem.at[CD])
    picture.start()

    def store(k):
        return pltpu.make_async_copy(buf.at[k], o_hbm.at[k], out_sem.at[k])

    for k in range(CD):
        for e in range(SLABS):
            rows = pl.ds(ROWS * e, ROWS)
            buf[k, rows, :] = g_ref[k, rows, :] - q_ref[e]
        store(k).start()
    for k in range(CD):
        store(k).wait()
    picture.wait()


def on_device(
    thermal_field,
    particulate_fraction,
    sootiness_extinction,
    vapour_extinction_rate,
    planck_over_wavelength,
    layer_sightline_position,
    picture_adjoint_seed,
):
    smem = pl.BlockSpec(memory_space=pltpu.SMEM)
    vmem = pl.BlockSpec(memory_space=pltpu.VMEM)
    hbm = pl.BlockSpec(memory_space=pl.ANY)

    def v(*shape):
        return pltpu.VMEM(shape, F32)

    def sems(*shape):
        return pltpu.SemaphoreType.DMA(shape)

    field = (CD, LINES, LANES)
    image = (NB * ROWS, LANES)
    radiance, gradient, quot = pl.pallas_call(
        kernel,
        out_shape=(
            pltpu.VMEM((NB, 2, COLS * LANES), F32),
            pltpu.VMEM(field, F32),
            pltpu.VMEM((SLABS, ROWS, LANES), F32),
        ),
        in_specs=[smem, smem, smem, smem, hbm, hbm, hbm],
        out_specs=(vmem, vmem, vmem),
        scratch_shapes=[
            v(*field),
            pltpu.VMEM(field, jnp.bfloat16),
            v(*field),
            v(NB, *field),
            v(3, NB, *TILE),
            v(SLABS, 2, ROWS, LANES),
            v(SLABS, 2, ROWS, LANES),
            v(SLABS, 2, ROWS, LANES),
            v(SLABS, 2, ROWS, LANES),
            v(COLS, NB, 2, LANES),
            v(SLABS, *image),
            v(SLABS, *image),
            v(CHIPS, *image),
            v(3, *image),
            v(CHIPS, *image),
            v(SLABS, ROWS, LANES),
            v(SLABS, ROWS, LANES),
            v(SLABS, ROWS, LANES),
            v(SLABS, ROWS, LANES),
            v(*image),
            v(COLS, NB, 2, LANES),
            v(NB, 2, COLS * LANES),
            sems(2, CHIPS),
            sems(SLABS + 1),
            sems(SLABS),
            sems(SLABS),
            sems(SLABS),
            sems(SLABS),
            sems(COLS),
            sems(COLS),
            sems(SLABS),
            sems(SLABS),
            sems(SLABS),
            sems(SLABS),
            sems(CHIPS),
            sems(CHIPS),
            sems(3),
            sems(CHIPS),
            sems(SLABS),
            sems(SLABS),
            sems(SLABS),
            sems(SLABS),
            sems(COLS),
            sems(COLS),
        ],
        compiler_params=pltpu.CompilerParams(
            collective_id=0, has_side_effects=True, vmem_limit_bytes=56 << 20
        ),
    )(
        sootiness_extinction,
        vapour_extinction_rate,
        planck_over_wavelength,
        layer_sightline_position,
        thermal_field,
        particulate_fraction,
        picture_adjoint_seed,
    )
    gradient, radiance = pl.pallas_call(
        subtract_kernel,
        out_shape=(
            jax.ShapeDtypeStruct(field, F32),
            jax.ShapeDtypeStruct((NB, 2, COLS * LANES), F32),
        ),
        in_specs=[vmem, vmem, vmem],
        out_specs=(hbm, hbm),
        scratch_shapes=[v(*field), sems(CD + 1)],
        compiler_params=pltpu.CompilerParams(vmem_limit_bytes=8 << 20),
    )(quot, gradient, radiance)
    return radiance, gradient


def solution(mesh):
    placed = (
        P("depth", None, "width"),
        P("depth", None, "width"),
        P(),
        P(),
        P(),
        P(),
        P(None, ("depth", "width"), None),
    )
    return jax.shard_map(
        on_device,
        mesh=mesh,
        in_specs=placed,
        out_specs=(P(None, ("depth", "width"), None), P("depth", None, "width")),
        check_vma=False,
    )
```
